256 devices in a mesh: rep: 4 (over y), exp: 64 (over z, x, core).
Axes of the slice: x: 4, y: 4, z: 8, core: 2. Of those that a mesh axis runs over, the one named last changes fastest.
Arguments:
- cache_keys: bfloat16 [256, 2048, 512], P(('rep', 'exp')), may hold values from -6.5 to 6.5
- cache_values: bfloat16 [256, 2048, 512], P(('rep', 'exp')), may hold values from -6 to 6
- lengths: int32 [256], P(('rep', 'exp')), may hold values from 512 to 2048, as said below
- drift_rows: int32 [2, 256, 8], P(None, ('rep', 'exp')), may hold values from 0 to 2047, as said below
- block_in: bfloat16 [256, 8, 4096], P(('rep', 'exp')), may hold values from -6 to 6
- drift_in: bfloat16 [2, 256, 8, 4096], P(None, ('rep', 'exp')), may hold values from -6 to 6
- queries: bfloat16 [2, 256, 16, 4096], P(None, ('rep', 'exp')), may hold values from -150 to 150
- new_keys: bfloat16 [2, 256, 16, 512], P(None, ('rep', 'exp')), may hold values from -6 to 6
- new_values: bfloat16 [2, 256, 16, 512], P(None, ('rep', 'exp')), may hold values from -6 to 6
- norm_gain: float32 [4096], replicated, may hold values from 0.25 to 1.75
- expert_ids: int32 [2, 256, 16, 8], P(None, ('rep', 'exp')), may hold values from 0 to 63, all different within a row; in each aligned block of 16 rows (0 to 15, 16 to 31, ..., all dimensions but the last counted through in order) at most 3 rows name the same one
- gate_weights: bfloat16 [2, 256, 16, 8], P(None, ('rep', 'exp')), may hold values from 0.049804688 to 0.3984375
- w_gate: bfloat16 [64, 4096, 1024], P('exp', None, 'rep'), may hold values from -0.09375 to 0.09375
- w_up: bfloat16 [64, 4096, 1024], P('exp', None, 'rep'), may hold values from -0.09375 to 0.09375
- w_down: bfloat16 [64, 1024, 4096], P('exp', 'rep'), may hold values from -0.1875 to 0.1875
Outputs:
- out: bfloat16 [2, 256, 16, 4096], P(None, ('rep', 'exp'))
The draws below stay inside these ranges and needn't reach their ends.
Inputs may be any that keep to these rules, and one draw needn't show every extreme that they name: `lengths`: one request has exactly 2048. `drift_rows`: for each step and request, 8 different positions in increasing order, all below that request's length. `expert_ids`: each row names 8 different experts; within one step the rows of one request name any expert at most 3 times, a bound that some block reaches.
All inputs are finite; a program needn't handle non-finite values.
Results may differ from the reference program's by a relative error of at most 0.012.
Values may be sent and summed in bfloat16 or wider, within the bound.
No kernel may reach another device: no remote copies, remote signals or barrier semaphores. Data moves between devices by JAX's collectives and lax.ppermute only.
A program may use at most 128 MiB of HBM per device.

```python
import math
import jax
import jax.numpy as jnp
import numpy as np
from jax import lax

D = 4096
H = 32
KVH = 4
HD = 128
FFE = 1024
TOP = 8
BLOCK = 8
DRIFT = 8
CACHE = 2048
ROWS = 16
REQUESTS = 256
EXPERTS = 64
CAP = 3
N_REP = 4


def length_table(key):
    lengths_drawn = jax.random.randint(jax.random.fold_in(key, 11), (REQUESTS,), CACHE // 4, CACHE + 1)
    longest = jax.random.randint(jax.random.fold_in(key, 12), (), 0, REQUESTS)
    return jnp.where(jnp.arange(REQUESTS) == longest, CACHE, lengths_drawn).astype(jnp.int32)


def draw_lengths(key, part):
    return length_table(key)


def draw_drift_rows(key, part):
    length_all = length_table(key)
    offsets = jax.random.randint(jax.random.fold_in(key, 13), (2, REQUESTS, DRIFT), 0, 1048576)
    stratum = jnp.arange(DRIFT)[None, None, :]
    stratum_low = length_all[None, :, None] * stratum // DRIFT
    stratum_high = length_all[None, :, None] * (stratum + 1) // DRIFT
    return (stratum_low + offsets % (stratum_high - stratum_low)).astype(jnp.int32)


def key_table(key):
    normal_draw = jax.random.normal(jax.random.fold_in(key, 21), (REQUESTS, CACHE, KVH * HD), jnp.float32)
    normal_draw = jnp.clip(normal_draw, -6.0, 6.0)
    return normal_draw


def draw_cache_keys(key, part):
    return key_table(key).astype(jnp.bfloat16)


def draw_queries(key, part):
    normal_draw = jax.random.normal(jax.random.fold_in(key, 31), (2, REQUESTS, ROWS, H * HD), jnp.float32)
    normal_draw = jnp.clip(normal_draw, -6.0, 6.0)
    return normal_draw.astype(jnp.bfloat16)


def level_of(rng, extent, split, least, high):
    level = 1.0
    for dim, shards_of in split:
        heights = jax.random.uniform(jax.random.fold_in(jax.random.fold_in(rng, 6), dim), (shards_of,), jnp.float32, least / len(split), high / len(split))
        level = level * jnp.repeat(jnp.exp(heights), extent[dim] // shards_of).reshape((-1,) + (1,) * (len(extent) - 1 - dim))
    return level


def assign_block(rng, own, number, rows, count, top, limit, skew):
    sequence = jax.random.permutation(rng, count)
    heavy_load, usual = portions_of(count, rows * top, limit, skew, True), portions_of(count, rows * top, limit, skew, False)
    places = jnp.arange(count)

    def named(sizes, rotation):
        used = int((sizes > 0).sum())
        fixed = max(1, used // 4)
        moved = fixed + (places - fixed + rotation * (used - fixed)) % max(1, count - fixed)
        return jnp.zeros((count,), jnp.int32).at[sequence[jnp.where(places < fixed, places, moved)]].set(jnp.asarray(sizes, jnp.int32))

    sizes = jnp.where(number % 4 == 0, named(heavy_load, number // 4), named(usual, number - number // 4 - 1))
    mixed = jax.random.permutation(jax.random.fold_in(own, 3), count)
    source_of, taker = mixed[0:count // 2 * 2:2], mixed[1:count // 2 * 2:2]
    margin = jnp.minimum(sizes[source_of] - 1, limit - sizes[taker]) // 2
    margin = jnp.where((source_of == sequence[0]) | (taker == sequence[0]) | (sizes[taker] == 0), 0, jnp.maximum(margin, 0))
    moved = jax.random.randint(jax.random.fold_in(own, 4), (count // 2,), 0, 1 << 20) % (margin + 1)
    sizes = sizes.at[source_of].add(-moved).at[taker].add(moved)
    labels = jnp.searchsorted(jnp.cumsum(sizes), jnp.arange(rows * top), side="right").astype(jnp.int32)
    grid = labels.reshape(top, rows).T
    grid = grid[jax.random.permutation(jax.random.fold_in(own, 1), rows)]
    rotation = jax.random.randint(jax.random.fold_in(own, 2), (rows, 1), 0, top)
    return jnp.take_along_axis(grid, (jnp.arange(top)[None, :] + rotation) % top, axis=1)


def portions_of(count, total, bound, skew, full):
    weights = [(1 << 20) // math.isqrt(standing ** skew) + 1 for standing in range(1, count + 1)]
    largest = bound if full else min(bound, max(-(-total // count), total * weights[0] // sum(weights)))
    least = 1 if total - largest >= count - 1 else 0
    given, surplus = [largest] + [least] * (count - 1), total - largest - least * (count - 1)
    while surplus > 0:
        free = [i for i in range(1, count) if given[i] < largest] or [i for i in range(1, count) if given[i] < bound]
        mass, budget = sum([weights[i] for i in free]), surplus
        for i in free:
            more = min(bound - given[i], max(1, budget * weights[i] // mass), surplus)
            given[i] = given[i] + more
            surplus = surplus - more
    return np.array(given)


def bell_draw(rng, shape, scale, reach, shards=(), dtype=jnp.bfloat16):
    values = jax.random.normal(rng, shape, jnp.float32) * scale
    if len(shards) > 0:
        values = level_of(rng, shape, shards, -0.22, 0.18) * values
    return jnp.clip(values, min=-reach, max=reach).astype(dtype)


def setup_inputs(seed: int = 0) -> dict:
    arg_keys = jax.random.split(jax.random.key(seed), 16)
    cache_keys = draw_cache_keys(jax.random.fold_in(arg_keys[15], 71), 0)
    cache_values = bell_draw(arg_keys[1], (REQUESTS, CACHE, KVH * HD), 1.0, 6.0, ((0, 256),))
    lengths = draw_lengths(jax.random.fold_in(arg_keys[15], 71), 0)
    drift_rows = draw_drift_rows(jax.random.fold_in(arg_keys[15], 71), 0)
    block_in = bell_draw(arg_keys[4], (REQUESTS, BLOCK, D), 1.0, 6.0, ((0, 256),))
    drift_in = bell_draw(arg_keys[5], (2, REQUESTS, DRIFT, D), 1.0, 6.0, ((1, 256),))
    queries = draw_queries(jax.random.fold_in(arg_keys[15], 71), 0)
    new_keys = bell_draw(arg_keys[7], (2, REQUESTS, ROWS, KVH * HD), 1.0, 6.0, ((1, 256),))
    new_values = bell_draw(arg_keys[8], (2, REQUESTS, ROWS, KVH * HD), 1.0, 6.0, ((1, 256),))
    norm_gain = jnp.clip(1.0 + 0.15 * jax.random.normal(arg_keys[9], (D,), jnp.float32), 0.25, 1.75)
    expert_ids_keys = jax.random.split(jax.random.fold_in(arg_keys[10], 1), 2 * REQUESTS * ROWS // ROWS)
    expert_ids_turns = jax.random.permutation(jax.random.fold_in(arg_keys[10], 3), 2 * REQUESTS * ROWS // ROWS)
    expert_ids = jax.vmap(lambda own, number: assign_block(jax.random.fold_in(arg_keys[10], 2), own, number, ROWS, EXPERTS, TOP, CAP, 2))(expert_ids_keys, expert_ids_turns).reshape((2, REQUESTS, ROWS, TOP))
    gate_weights = jnp.clip(0.049804688 + 0.3486328 * jax.random.uniform(arg_keys[11], (2, REQUESTS, ROWS, TOP), jnp.float32) ** level_of(arg_keys[11], (2, REQUESTS, ROWS, TOP), ((1, 256),), -0.2, 0.2), 0.049804688, 0.3984375).astype(jnp.bfloat16)
    w_gate = bell_draw(arg_keys[12], (EXPERTS, D, FFE), D ** -0.5, 0.09375, ((0, 64), (2, 4)))
    w_up = bell_draw(arg_keys[13], (EXPERTS, D, FFE), D ** -0.5, 0.09375, ((0, 64), (2, 4)))
    w_down = bell_draw(arg_keys[14], (EXPERTS, FFE, D), FFE ** -0.5, 0.1875, ((0, 64), (1, 4)))
    return dict(cache_keys=cache_keys, cache_values=cache_values, lengths=lengths, drift_rows=drift_rows, block_in=block_in, drift_in=drift_in, queries=queries, new_keys=new_keys, new_values=new_values, norm_gain=norm_gain, expert_ids=expert_ids, gate_weights=gate_weights, w_gate=w_gate, w_up=w_up, w_down=w_down)


def attend(query_rows, key_rows, value_rows, block_keys, block_values, length):
    row_count = query_rows.shape[0]
    group_size = H // KVH
    query_head_rows = query_rows.astype(jnp.float32).reshape(row_count, KVH, group_size, HD)
    cache_k = key_rows.astype(jnp.float32).reshape(-1, KVH, HD)
    cached_value_rows = value_rows.astype(jnp.float32).reshape(-1, KVH, HD)
    prompt_key_rows = block_keys.astype(jnp.float32).reshape(-1, KVH, HD)
    prompt_value_rows = block_values.astype(jnp.float32).reshape(-1, KVH, HD)
    logit_scale_factor = HD ** (-0.5)
    cache_scores = jnp.einsum('rkgd,ckd->kgrc', query_head_rows, cache_k) * logit_scale_factor
    prompt_score_rows = jnp.einsum('afhu,nfu->fhan', query_head_rows, prompt_key_rows) * logit_scale_factor
    cache_mask = jnp.arange(cache_k.shape[0]) < length
    own_mask = (jnp.arange(row_count) < BLOCK)[:, None]
    cache_scores = jnp.where(cache_mask, cache_scores, -1e+30)
    prompt_score_rows = jnp.where(own_mask, prompt_score_rows, -1e+30)
    peak = jnp.maximum(lax.optimization_barrier(jnp.max(cache_scores, axis=-1)), lax.optimization_barrier(jnp.max(prompt_score_rows, axis=-1)))
    cache_exp = jnp.exp(cache_scores - peak[..., None])
    own_exp = jnp.exp(prompt_score_rows - peak[..., None])
    denom = lax.optimization_barrier(jnp.sum(cache_exp, axis=-1)) + lax.optimization_barrier(jnp.sum(own_exp, axis=-1))
    cached_weight_share = (cache_exp / denom[..., None]).astype(jnp.bfloat16).astype(jnp.float32)
    prompt_weight_share = (own_exp / denom[..., None]).astype(jnp.bfloat16).astype(jnp.float32)
    blended_output = jnp.einsum('qimt,tqj->mqij', cached_weight_share, cached_value_rows) + jnp.einsum('iywf,fie->wiye', prompt_weight_share, prompt_value_rows)
    return blended_output.reshape(row_count, H * HD)

def route_table(routed, gate_share):
    member = routed[:, :, None] == jnp.arange(EXPERTS)[None, None, :]
    weight = lax.optimization_barrier(jnp.sum(jnp.where(member, gate_share[:, :, None].astype(jnp.float32), 0.0), axis=1))
    chosen = jnp.any(member, axis=1).astype(jnp.int32)
    slot_rank = jnp.cumsum(chosen, axis=0) - chosen
    taken = (slot_rank[:, :, None] == jnp.arange(CAP)[None, None, :]) & (chosen[:, :, None] == 1)
    return jnp.where(taken, weight[:, :, None], 0.0).astype(jnp.bfloat16)

def mixture(normed, tables, w_gate, w_up, w_down):
    quarter = FFE // N_REP

    def add_expert(running, expert):
        slot_table = lax.dynamic_index_in_dim(tables, expert, axis=2, keepdims=False)
        chosen = (slot_table != 0).astype(jnp.float32)
        dispatched = jnp.einsum('rjc,rjd->rcd', chosen, normed.astype(jnp.float32))
        flat_rows = dispatched.reshape(-1, D).astype(jnp.bfloat16)
        gate_act = jnp.dot(flat_rows, w_gate[expert], preferred_element_type=jnp.float32)
        up_act = jnp.dot(flat_rows, w_up[expert], preferred_element_type=jnp.float32)
        hidden = (jax.nn.silu(gate_act) * up_act).astype(jnp.bfloat16)
        down_rows = w_down[expert]
        summed = jnp.zeros((flat_rows.shape[0], D), jnp.float32)
        for index in range(N_REP):
            part_out = jnp.dot(hidden[:, index * quarter:(index + 1) * quarter], down_rows[index * quarter:(index + 1) * quarter], preferred_element_type=jnp.float32).astype(jnp.bfloat16)
            summed = summed + lax.optimization_barrier(part_out).astype(jnp.float32)
        summed = summed.reshape(REQUESTS, CAP, D)
        running = running + jnp.einsum('rjc,rcd->rjd', slot_table.astype(jnp.float32), summed)
        return (running, None)
    start = jnp.zeros((REQUESTS, ROWS, D), jnp.float32)
    running, _ = lax.scan(add_expert, start, jnp.arange(EXPERTS).astype(jnp.int32))
    return running

def reference(cache_keys, cache_values, lengths, drift_rows, block_in, drift_in, queries, new_keys, new_values, norm_gain, expert_ids, gate_weights, w_gate, w_up, w_down):
    outputs = []
    carried = block_in
    drift_by_req = jnp.swapaxes(drift_rows, 0, 1)
    query_by_req = jnp.swapaxes(queries, 0, 1)
    keys_by_req = jnp.swapaxes(new_keys, 0, 1)
    values_by_req = jnp.swapaxes(new_values, 0, 1)
    for denoise in range(2):

        def per_request(packed):
            key_rows, value_rows, length, drifts, query_rows, fresh_k, fresh_v = packed
            for past in range(denoise + 1):
                key_rows = key_rows.at[drifts[past]].set(fresh_k[past, BLOCK:])
                value_rows = value_rows.at[drifts[past]].set(fresh_v[past, BLOCK:])
            return attend(query_rows[denoise], key_rows, value_rows, fresh_k[denoise, :BLOCK], fresh_v[denoise, :BLOCK], length)
        attended = lax.map(per_request, (cache_keys, cache_values, lengths, drift_by_req, query_by_req, keys_by_req, values_by_req))
        inputs = jnp.concatenate([carried, drift_in[denoise]], axis=1).astype(jnp.float32)
        residual = inputs + attended
        inverse = lax.rsqrt(lax.optimization_barrier(jnp.mean(residual * residual, axis=-1, keepdims=True)) + 1e-06)
        normed = (residual * inverse * norm_gain).astype(jnp.bfloat16)
        tables = jax.vmap(route_table)(expert_ids[denoise], gate_weights[denoise])
        moe = mixture(normed, tables, w_gate, w_up, w_down)
        result = (residual + moe).astype(jnp.bfloat16)
        outputs.append(result)
        carried = result[:, :BLOCK]
    return jnp.stack(outputs)
```

```python
import jax
import jax.numpy as jnp
from jax import lax
from jax.experimental import pallas as pl
from jax.experimental.pallas import tpu as pltpu
from jax.sharding import PartitionSpec as P

H = 32
KVH = 4
GROUP = H // KVH
HD = 128
D = H * HD
TOP = 8
BLOCK = 8
ROWS = 16
CAP = 3
EXPERTS = 64
SLOTS = EXPERTS * CAP
CACHE = 2048
QUARTER = 256
NEG = -1e30
VMEM_LIMIT = 56 * 1024 * 1024


def smem_spec():
    return pl.BlockSpec(memory_space=pltpu.SMEM)


def each_slot(ids_ref, denoise, counts, visit):
    for e in range(EXPERTS):
        counts[e] = 0

    @pl.loop(0, ROWS)
    def _(t):
        picked = []
        for j in range(TOP):
            e = ids_ref[denoise, 0, t, j]
            c = counts[e]
            counts[e] = c + 1
            picked.append(e * CAP + jnp.minimum(c, CAP - 1))
        visit(t, picked)


def normalize(residual, gain):
    inverse = lax.rsqrt(jnp.mean(residual * residual, axis=-1, keepdims=True) + 1e-06)
    return residual * inverse * gain


def dispatch(normed, ids_ref, denoise, counts, spread, packed, send_ref):
    for k in range(H):
        spread[pl.ds(k, ROWS, stride=H), :] = normed[:, k * HD : (k + 1) * HD]
    packed[...] = spread[...].reshape(ROWS, H, HD).astype(jnp.bfloat16)
    send_ref[...] = jnp.zeros_like(send_ref)

    def visit(t, picked):
        row = packed[t]
        for slot in picked:
            send_ref[slot] = row

    each_slot(ids_ref, denoise, counts, visit)


def combine(terms_ref, ids_ref, gates_ref, denoise, counts, spread):
    def visit(t, picked):
        total = jnp.zeros((H, HD), jnp.float32)
        for j, slot in enumerate(picked):
            total = total + gates_ref[denoise, 0, t, j] * terms_ref[slot].astype(jnp.float32)
        spread[pl.ds(pl.multiple_of(t * H, H), H), :] = total

    each_slot(ids_ref, denoise, counts, visit)
    return jnp.concatenate([spread[pl.ds(k, ROWS, stride=H), :] for k in range(H)], axis=1)


def attend_head(denoise, lengths_ref, drift_ref, q_ref, k_ref, v_ref, nk_ref, nv_ref, bias, attended):
    head = pl.program_id(0)
    extra = ROWS * (denoise + 1)

    @pl.when(head == 0)
    def _():
        place = lax.broadcasted_iota(jnp.int32, (1, CACHE), 1)
        admitted = place < lengths_ref[0]
        for step in range(denoise + 1):
            for b in range(BLOCK):
                admitted = admitted & (place != drift_ref[step, 0, b])
        bias[...] = jnp.where(admitted, 0.0, NEG)

    queries = jnp.concatenate([q_ref[:, g * HD : (g + 1) * HD] for g in range(GROUP)], axis=0)
    contract_last = (((1,), (1,)), ((), ()))
    scale = HD ** (-0.5)
    scores = lax.dot_general(queries, k_ref[...], contract_last, preferred_element_type=jnp.float32)
    scores = scores * scale + bias[...]
    fresh_k = nk_ref[0 : denoise + 1].reshape(extra, HD)
    fresh_v = nv_ref[0 : denoise + 1].reshape(extra, HD)
    fresh = lax.dot_general(queries, fresh_k, contract_last, preferred_element_type=jnp.float32)
    row = lax.broadcasted_iota(jnp.int32, (GROUP * ROWS, extra), 0)
    col = lax.broadcasted_iota(jnp.int32, (GROUP * ROWS, extra), 1)
    place = col % ROWS
    allowed = (col >= denoise * ROWS) & ((place >= BLOCK) | (row % ROWS < BLOCK))
    if denoise == 1:
        for b in range(BLOCK):
            kept = drift_ref[1, 0, 0] != drift_ref[0, 0, b]
            for other in range(1, BLOCK):
                kept = kept & (drift_ref[1, 0, other] != drift_ref[0, 0, b])
            allowed = allowed | ((col == BLOCK + b) & kept)
    fresh = jnp.where(allowed, fresh * scale, NEG)
    peak = jnp.maximum(
        jnp.max(scores, axis=-1, keepdims=True), jnp.max(fresh, axis=-1, keepdims=True)
    )
    scores = jnp.exp(scores - peak)
    fresh = jnp.exp(fresh - peak)
    denom = jnp.sum(scores, axis=-1, keepdims=True) + jnp.sum(fresh, axis=-1, keepdims=True)
    mixed = jnp.dot(scores.astype(jnp.bfloat16), v_ref[...], preferred_element_type=jnp.float32)
    mixed = mixed + jnp.dot(fresh.astype(jnp.bfloat16), fresh_v, preferred_element_type=jnp.float32)
    mixed = mixed / denom
    wide = jnp.concatenate([mixed[g * ROWS : (g + 1) * ROWS] for g in range(GROUP)], axis=1)
    attended[:, pl.ds(pl.multiple_of(head * GROUP * HD, GROUP * HD), GROUP * HD)] = wide


def attention_specs(denoise):
    return [
        smem_spec(),
        smem_spec(),
        pl.BlockSpec((None, None, ROWS, GROUP * HD), lambda h: (denoise, 0, 0, h)),
        pl.BlockSpec((None, CACHE, HD), lambda h: (0, 0, h)),
        pl.BlockSpec((None, CACHE, HD), lambda h: (0, 0, h)),
        pl.BlockSpec((2, None, ROWS, HD), lambda h: (0, 0, 0, h)),
        pl.BlockSpec((2, None, ROWS, HD), lambda h: (0, 0, 0, h)),
    ]


def first_attention(lengths, drift_rows, queries, keys, values, new_keys, new_values, block_in, drift_in, gain, ids):
    def body(lengths_ref, drift_ref, q_ref, k_ref, v_ref, nk_ref, nv_ref, block_ref, drift_in_ref, gain_ref, ids_ref,
             residual_ref, send_ref, bias, attended, spread, packed, counts):
        attend_head(0, lengths_ref, drift_ref, q_ref, k_ref, v_ref, nk_ref, nv_ref, bias, attended)

        @pl.when(pl.program_id(0) == KVH - 1)
        def _():
            inputs = jnp.concatenate(
                [block_ref[...].astype(jnp.float32), drift_in_ref[...].astype(jnp.float32)], axis=0
            )
            residual = inputs + attended[...]
            residual_ref[...] = residual
            dispatch(normalize(residual, gain_ref[...]), ids_ref, 0, counts, spread, packed, send_ref)

    return pl.pallas_call(
        body,
        grid=(KVH,),
        in_specs=attention_specs(0)
        + [
            pl.BlockSpec((None, BLOCK, D), lambda h: (0, 0, 0)),
            pl.BlockSpec((None, None, BLOCK, D), lambda h: (0, 0, 0, 0)),
            pl.BlockSpec((1, D), lambda h: (0, 0)),
            smem_spec(),
        ],
        out_specs=[
            pl.BlockSpec((ROWS, D), lambda h: (0, 0)),
            pl.BlockSpec((SLOTS, H, HD), lambda h: (0, 0, 0)),
        ],
        out_shape=[
            jax.ShapeDtypeStruct((ROWS, D), jnp.float32),
            jax.ShapeDtypeStruct((SLOTS, H, HD), jnp.bfloat16),
        ],
        scratch_shapes=[
            pltpu.VMEM((1, CACHE), jnp.float32),
            pltpu.VMEM((ROWS, D), jnp.float32),
            pltpu.VMEM((ROWS * H, HD), jnp.float32),
            pltpu.VMEM((ROWS, H, HD), jnp.bfloat16),
            pltpu.SMEM((EXPERTS,), jnp.int32),
        ],
        compiler_params=pltpu.CompilerParams(vmem_limit_bytes=VMEM_LIMIT),
        name="first_attention",
    )(lengths, drift_rows, queries, keys, values, new_keys, new_values, block_in, drift_in, gain, ids)


def second_attention(lengths, drift_rows, queries, keys, values, new_keys, new_values):
    def body(lengths_ref, drift_ref, q_ref, k_ref, v_ref, nk_ref, nv_ref, attended, bias):
        attend_head(1, lengths_ref, drift_ref, q_ref, k_ref, v_ref, nk_ref, nv_ref, bias, attended)

    return pl.pallas_call(
        body,
        grid=(KVH,),
        in_specs=attention_specs(1),
        out_specs=pl.BlockSpec((ROWS, D), lambda h: (0, 0)),
        out_shape=jax.ShapeDtypeStruct((ROWS, D), jnp.float32),
        scratch_shapes=[pltpu.VMEM((1, CACHE), jnp.float32)],
        compiler_params=pltpu.CompilerParams(vmem_limit_bytes=VMEM_LIMIT),
        name="second_attention",
    )(lengths, drift_rows, queries, keys, values, new_keys, new_values)


def expert_half(rows, weights):
    pieces = len(weights) // 3

    def body(*refs):
        rows_ref = refs[0]
        weight_refs = refs[1 : 1 + 3 * pieces]
        out_ref = refs[1 + 3 * pieces]
        gate, up, down, spread, flat, hidden, sems = refs[2 + 3 * pieces :]
        copies = []
        for p in range(pieces):
            for kind, target in enumerate((gate, up, down)):
                copies.append(
                    pltpu.make_async_copy(
                        weight_refs[3 * p + kind], target.at[p], sems.at[3 * p + kind]
                    )
                )
        for copy in copies:
            copy.start()
        spread[...] = rows_ref[...].reshape(SLOTS * H, HD).astype(jnp.float32)
        for k in range(H):
            flat[:, k * HD : (k + 1) * HD] = spread[pl.ds(k, SLOTS, stride=H), :].astype(jnp.bfloat16)
        for p in range(pieces):
            copies[3 * p].wait()
            gated = jnp.dot(flat[...], gate[p], preferred_element_type=jnp.float32)
            copies[3 * p + 1].wait()
            raised = jnp.dot(flat[...], up[p], preferred_element_type=jnp.float32)
            hidden[p] = (jax.nn.silu(gated) * raised).astype(jnp.bfloat16)
        for p in range(pieces):
            copies[3 * p + 2].wait()
        width = 512
        for n in range(D // width):
            part = jnp.zeros((SLOTS, width), jnp.float32)
            for p in range(pieces):
                part = part + jnp.dot(
                    hidden[p], down[p, :, n * width : (n + 1) * width], preferred_element_type=jnp.float32
                )
            for k in range(width // HD):
                spread[pl.ds(n * (width // HD) + k, SLOTS, stride=H), :] = part[:, k * HD : (k + 1) * HD]
        out_ref[...] = spread[...].reshape(SLOTS, H, HD).astype(jnp.bfloat16)

    return pl.pallas_call(
        body,
        in_specs=[pl.BlockSpec(memory_space=pltpu.VMEM)] + [pl.BlockSpec(memory_space=pl.ANY)] * (3 * pieces),
        out_specs=pl.BlockSpec(memory_space=pltpu.VMEM),
        out_shape=jax.ShapeDtypeStruct((SLOTS, H, HD), jnp.bfloat16),
        scratch_shapes=[
            pltpu.VMEM((pieces, D, QUARTER), jnp.bfloat16),
            pltpu.VMEM((pieces, D, QUARTER), jnp.bfloat16),
            pltpu.VMEM((pieces, QUARTER, D), jnp.bfloat16),
            pltpu.VMEM((SLOTS * H, HD), jnp.float32),
            pltpu.VMEM((SLOTS, D), jnp.bfloat16),
            pltpu.VMEM((pieces, SLOTS, QUARTER), jnp.bfloat16),
            pltpu.SemaphoreType.DMA((3 * pieces,)),
        ],
        compiler_params=pltpu.CompilerParams(vmem_limit_bytes=VMEM_LIMIT),
        name="expert_half",
    )(rows, *weights)


def combine_and_dispatch(terms, residual, attended, drift_in, gain, ids, gates):
    def body(terms_ref, residual_ref, attended_ref, drift_in_ref, gain_ref, ids_ref, gates_ref,
             result_ref, next_ref, send_ref, spread, packed, counts):
        moe = combine(terms_ref, ids_ref, gates_ref, 0, counts, spread)
        result = (residual_ref[...] + moe).astype(jnp.bfloat16)
        result_ref[...] = result
        inputs = jnp.concatenate(
            [result.astype(jnp.float32)[:BLOCK], drift_in_ref[1, 0].astype(jnp.float32)], axis=0
        )
        following = inputs + attended_ref[...]
        next_ref[...] = following
        dispatch(normalize(following, gain_ref[...]), ids_ref, 1, counts, spread, packed, send_ref)

    vmem = pl.BlockSpec(memory_space=pltpu.VMEM)
    return pl.pallas_call(
        body,
        in_specs=[vmem] * 5 + [smem_spec()] * 2,
        out_specs=[vmem] * 3,
        out_shape=[
            jax.ShapeDtypeStruct((ROWS, D), jnp.bfloat16),
            jax.ShapeDtypeStruct((ROWS, D), jnp.float32),
            jax.ShapeDtypeStruct((SLOTS, H, HD), jnp.bfloat16),
        ],
        scratch_shapes=[
            pltpu.VMEM((ROWS * H, HD), jnp.float32),
            pltpu.VMEM((ROWS, H, HD), jnp.bfloat16),
            pltpu.SMEM((EXPERTS,), jnp.int32),
        ],
        compiler_params=pltpu.CompilerParams(vmem_limit_bytes=VMEM_LIMIT),
        name="combine_and_dispatch",
    )(terms, residual, attended, drift_in, gain, ids, gates)


def combine_last(terms, residual, first_result, ids, gates):
    def body(terms_ref, residual_ref, first_ref, ids_ref, gates_ref, out_ref, spread, counts):
        moe = combine(terms_ref, ids_ref, gates_ref, 1, counts, spread)
        out_ref[0, 0] = first_ref[...]
        out_ref[1, 0] = (residual_ref[...] + moe).astype(jnp.bfloat16)

    vmem = pl.BlockSpec(memory_space=pltpu.VMEM)
    return pl.pallas_call(
        body,
        in_specs=[vmem] * 3 + [smem_spec()] * 2,
        out_specs=vmem,
        out_shape=jax.ShapeDtypeStruct((2, 1, ROWS, D), jnp.bfloat16),
        scratch_shapes=[
            pltpu.VMEM((ROWS * H, HD), jnp.float32),
            pltpu.SMEM((EXPERTS,), jnp.int32),
        ],
        compiler_params=pltpu.CompilerParams(vmem_limit_bytes=VMEM_LIMIT),
        name="combine_last",
    )(terms, residual, first_result, ids, gates)


def pairings(reps, exps):
    across, beside = [], []
    for r in range(reps):
        for e in range(exps):
            near, far = r ^ 1, reps - 1 - r
            if e % 2:
                near, far = far, near
            beside.append((r * exps + e, near * exps + e))
            across.append((r * exps + e, far * exps + e))
    return beside, across


def on_device(
    cache_keys,
    cache_values,
    lengths,
    drift_rows,
    block_in,
    drift_in,
    queries,
    new_keys,
    new_values,
    norm_gain,
    expert_ids,
    gate_weights,
    w_gate,
    w_up,
    w_down,
):
    axes = ("rep", "exp")
    beside, across = pairings(lax.axis_size("rep"), lax.axis_size("exp"))
    own = (w_gate[0], w_up[0], w_down[0])
    paired = tuple(lax.ppermute(part, axes, beside) for part in own)
    weights = own + paired
    gain = norm_gain.reshape(1, D)
    gates = gate_weights.astype(jnp.float32)

    residual, send = first_attention(
        lengths, drift_rows, queries, cache_keys, cache_values, new_keys, new_values,
        block_in, drift_in, gain, expert_ids,
    )
    attended = second_attention(
        lengths, drift_rows, queries, cache_keys, cache_values, new_keys, new_values
    )

    def experts(send):
        rows = lax.all_to_all(send, "exp", split_axis=0, concat_axis=0, tiled=True)
        visiting = lax.ppermute(rows, axes, across)
        home_terms = expert_half(rows, weights)
        away_terms = lax.ppermute(expert_half(visiting, weights), axes, across)
        terms = (home_terms.astype(jnp.float32) + away_terms.astype(jnp.float32)).astype(jnp.bfloat16)
        return lax.all_to_all(terms, "exp", split_axis=0, concat_axis=0, tiled=True)

    terms = experts(send)
    result, residual, send = combine_and_dispatch(
        terms, residual, attended, drift_in, gain, expert_ids, gates
    )
    terms = experts(send)
    return combine_last(terms, residual, result, expert_ids, gates)


def solution(mesh):
    placed = (
        P(("rep", "exp"), None, None),
        P(("rep", "exp"), None, None),
        P(("rep", "exp")),
        P(None, ("rep", "exp"), None),
        P(("rep", "exp"), None, None),
        P(None, ("rep", "exp"), None, None),
        P(None, ("rep", "exp"), None, None),
        P(None, ("rep", "exp"), None, None),
        P(None, ("rep", "exp"), None, None),
        P(),
        P(None, ("rep", "exp"), None, None),
        P(None, ("rep", "exp"), None, None),
        P("exp", None, "rep"),
        P("exp", None, "rep"),
        P("exp", "rep", None),
    )
    return jax.shard_map(
        on_device,
        mesh=mesh,
        in_specs=placed,
        out_specs=P(None, ("rep", "exp"), None, None),
        check_vma=False,
    )
```

```python
import jax
import jax.numpy as jnp
from jax import lax
from jax.experimental import pallas as pl
from jax.experimental.pallas import tpu as pltpu
from jax.sharding import PartitionSpec as P

H = 32
KVH = 4
GROUP = H // KVH
HD = 128
D = H * HD
TOP = 8
BLOCK = 8
ROWS = 16
CAP = 3
EXPERTS = 64
SLOTS = EXPERTS * CAP
CACHE = 2048
QUARTER = 256
NEG = -1e30
VMEM_LIMIT = 56 * 1024 * 1024


def smem_spec():
    return pl.BlockSpec(memory_space=pltpu.SMEM)


def each_slot(ids_ref, denoise, counts, visit):
    for e in range(EXPERTS):
        counts[e] = 0

    @pl.loop(0, ROWS)
    def _(t):
        picked = []
        for j in range(TOP):
            e = ids_ref[denoise, 0, t, j]
            c = counts[e]
            counts[e] = c + 1
            picked.append(e * CAP + jnp.minimum(c, CAP - 1))
        visit(t, picked)


def normalize(residual, gain):
    inverse = lax.rsqrt(jnp.mean(residual * residual, axis=-1, keepdims=True) + 1e-06)
    return residual * inverse * gain


def dispatch(normed, ids_ref, denoise, counts, spread, packed, send_ref):
    for k in range(H):
        spread[pl.ds(k, ROWS, stride=H), :] = normed[:, k * HD : (k + 1) * HD]
    packed[...] = spread[...].reshape(ROWS, H, HD).astype(jnp.bfloat16)
    send_ref[...] = jnp.zeros_like(send_ref)

    def visit(t, picked):
        row = packed[t]
        for slot in picked:
            send_ref[slot] = row

    each_slot(ids_ref, denoise, counts, visit)


def combine(terms_ref, ids_ref, gates_ref, denoise, counts, spread):
    def visit(t, picked):
        total = jnp.zeros((H, HD), jnp.float32)
        for j, slot in enumerate(picked):
            total = total + gates_ref[denoise, 0, t, j] * terms_ref[slot].astype(jnp.float32)
        spread[pl.ds(pl.multiple_of(t * H, H), H), :] = total

    each_slot(ids_ref, denoise, counts, visit)
    return jnp.concatenate([spread[pl.ds(k, ROWS, stride=H), :] for k in range(H)], axis=1)


def attend_head(denoise, lengths_ref, drift_ref, q_ref, k_ref, v_ref, nk_ref, nv_ref, bias, attended):
    head = pl.program_id(0)
    extra = ROWS * (denoise + 1)

    @pl.when(head == 0)
    def _():
        place = lax.broadcasted_iota(jnp.int32, (1, CACHE), 1)
        admitted = place < lengths_ref[0]
        for step in range(denoise + 1):
            for b in range(BLOCK):
                admitted = admitted & (place != drift_ref[step, 0, b])
        bias[...] = jnp.where(admitted, 0.0, NEG)

    queries = jnp.concatenate([q_ref[:, g * HD : (g + 1) * HD] for g in range(GROUP)], axis=0)
    contract_last = (((1,), (1,)), ((), ()))
    scale = HD ** (-0.5)
    scores = lax.dot_general(queries, k_ref[...], contract_last, preferred_element_type=jnp.float32)
    scores = scores * scale + bias[...]
    fresh_k = nk_ref[0 : denoise + 1].reshape(extra, HD)
    fresh_v = nv_ref[0 : denoise + 1].reshape(extra, HD)
    fresh = lax.dot_general(queries, fresh_k, contract_last, preferred_element_type=jnp.float32)
    row = lax.broadcasted_iota(jnp.int32, (GROUP * ROWS, extra), 0)
    col = lax.broadcasted_iota(jnp.int32, (GROUP * ROWS, extra), 1)
    place = col % ROWS
    allowed = (col >= denoise * ROWS) & ((place >= BLOCK) | (row % ROWS < BLOCK))
    if denoise == 1:
        for b in range(BLOCK):
            kept = drift_ref[1, 0, 0] != drift_ref[0, 0, b]
            for other in range(1, BLOCK):
                kept = kept & (drift_ref[1, 0, other] != drift_ref[0, 0, b])
            allowed = allowed | ((col == BLOCK + b) & kept)
    fresh = jnp.where(allowed, fresh * scale, NEG)
    peak = jnp.maximum(
        jnp.max(scores, axis=-1, keepdims=True), jnp.max(fresh, axis=-1, keepdims=True)
    )
    scores = jnp.exp(scores - peak)
    fresh = jnp.exp(fresh - peak)
    denom = jnp.sum(scores, axis=-1, keepdims=True) + jnp.sum(fresh, axis=-1, keepdims=True)
    mixed = jnp.dot(scores.astype(jnp.bfloat16), v_ref[...], preferred_element_type=jnp.float32)
    mixed = mixed + jnp.dot(fresh.astype(jnp.bfloat16), fresh_v, preferred_element_type=jnp.float32)
    mixed = mixed / denom
    wide = jnp.concatenate([mixed[g * ROWS : (g + 1) * ROWS] for g in range(GROUP)], axis=1)
    attended[:, pl.ds(pl.multiple_of(head * GROUP * HD, GROUP * HD), GROUP * HD)] = wide


def attention_specs(denoise):
    return [
        smem_spec(),
        smem_spec(),
        pl.BlockSpec((None, None, ROWS, GROUP * HD), lambda h: (denoise, 0, 0, h)),
        pl.BlockSpec((None, CACHE, HD), lambda h: (0, 0, h)),
        pl.BlockSpec((None, CACHE, HD), lambda h: (0, 0, h)),
        pl.BlockSpec((2, None, ROWS, HD), lambda h: (0, 0, 0, h)),
        pl.BlockSpec((2, None, ROWS, HD), lambda h: (0, 0, 0, h)),
    ]


def first_attention(lengths, drift_rows, queries, keys, values, new_keys, new_values, block_in, drift_in, gain, ids):
    def body(lengths_ref, drift_ref, q_ref, k_ref, v_ref, nk_ref, nv_ref, block_ref, drift_in_ref, gain_ref, ids_ref,
             residual_ref, send_ref, bias, attended, spread, packed, counts):
        attend_head(0, lengths_ref, drift_ref, q_ref, k_ref, v_ref, nk_ref, nv_ref, bias, attended)

        @pl.when(pl.program_id(0) == KVH - 1)
        def _():
            inputs = jnp.concatenate(
                [block_ref[...].astype(jnp.float32), drift_in_ref[...].astype(jnp.float32)], axis=0
            )
            residual = inputs + attended[...]
            residual_ref[...] = residual
            dispatch(normalize(residual, gain_ref[...]), ids_ref, 0, counts, spread, packed, send_ref)

    return pl.pallas_call(
        body,
        grid=(KVH,),
        in_specs=attention_specs(0)
        + [
            pl.BlockSpec((None, BLOCK, D), lambda h: (0, 0, 0)),
            pl.BlockSpec((None, None, BLOCK, D), lambda h: (0, 0, 0, 0)),
            pl.BlockSpec((1, D), lambda h: (0, 0)),
            smem_spec(),
        ],
        out_specs=[
            pl.BlockSpec((ROWS, D), lambda h: (0, 0)),
            pl.BlockSpec((SLOTS, H, HD), lambda h: (0, 0, 0)),
        ],
        out_shape=[
            jax.ShapeDtypeStruct((ROWS, D), jnp.float32),
            jax.ShapeDtypeStruct((SLOTS, H, HD), jnp.bfloat16),
        ],
        scratch_shapes=[
            pltpu.VMEM((1, CACHE), jnp.float32),
            pltpu.VMEM((ROWS, D), jnp.float32),
            pltpu.VMEM((ROWS * H, HD), jnp.float32),
            pltpu.VMEM((ROWS, H, HD), jnp.bfloat16),
            pltpu.SMEM((EXPERTS,), jnp.int32),
        ],
        compiler_params=pltpu.CompilerParams(vmem_limit_bytes=VMEM_LIMIT),
        name="first_attention",
    )(lengths, drift_rows, queries, keys, values, new_keys, new_values, block_in, drift_in, gain, ids)


def second_attention(lengths, drift_rows, queries, keys, values, new_keys, new_values):
    def body(lengths_ref, drift_ref, q_ref, k_ref, v_ref, nk_ref, nv_ref, attended, bias):
        attend_head(1, lengths_ref, drift_ref, q_ref, k_ref, v_ref, nk_ref, nv_ref, bias, attended)

    return pl.pallas_call(
        body,
        grid=(KVH,),
        in_specs=attention_specs(1),
        out_specs=pl.BlockSpec((ROWS, D), lambda h: (0, 0)),
        out_shape=jax.ShapeDtypeStruct((ROWS, D), jnp.float32),
        scratch_shapes=[pltpu.VMEM((1, CACHE), jnp.float32)],
        compiler_params=pltpu.CompilerParams(vmem_limit_bytes=VMEM_LIMIT),
        name="second_attention",
    )(lengths, drift_rows, queries, keys, values, new_keys, new_values)


def expert_half(rows, weights):
    pieces = len(weights) // 3

    def body(*refs):
        rows_ref = refs[0]
        weight_refs = refs[1 : 1 + 3 * pieces]
        out_ref = refs[1 + 3 * pieces]
        gate, up, down, flat, hidden, sems = refs[2 + 3 * pieces :]
        copies = []
        for p in range(pieces):
            for kind, target in enumerate((gate, up, down)):
                copies.append(
                    pltpu.make_async_copy(
                        weight_refs[3 * p + kind], target.at[p], sems.at[3 * p + kind]
                    )
                )
        for copy in copies:
            copy.start()
        for r in range(0, SLOTS, 16):
            wide = rows_ref[r : r + 16].astype(jnp.float32).reshape(16, D)
            flat[r : r + 16, :] = wide.astype(jnp.bfloat16)
        for p in range(pieces):
            copies[3 * p].wait()
            gated = jnp.dot(flat[...], gate[p], preferred_element_type=jnp.float32)
            copies[3 * p + 1].wait()
            raised = jnp.dot(flat[...], up[p], preferred_element_type=jnp.float32)
            hidden[p] = (jax.nn.silu(gated) * raised).astype(jnp.bfloat16)
        for p in range(pieces):
            copies[3 * p + 2].wait()
        width = 512
        for n in range(D // width):
            part = jnp.zeros((SLOTS, width), jnp.float32)
            for p in range(pieces):
                part = part + jnp.dot(
                    hidden[p], down[p, :, n * width : (n + 1) * width], preferred_element_type=jnp.float32
                )
            heads = width // HD
            out_ref[:, n * heads : (n + 1) * heads, :] = part.reshape(SLOTS, heads, HD).astype(jnp.bfloat16)

    return pl.pallas_call(
        body,
        in_specs=[pl.BlockSpec(memory_space=pltpu.VMEM)] + [pl.BlockSpec(memory_space=pl.ANY)] * (3 * pieces),
        out_specs=pl.BlockSpec(memory_space=pltpu.VMEM),
        out_shape=jax.ShapeDtypeStruct((SLOTS, H, HD), jnp.bfloat16),
        scratch_shapes=[
            pltpu.VMEM((pieces, D, QUARTER), jnp.bfloat16),
            pltpu.VMEM((pieces, D, QUARTER), jnp.bfloat16),
            pltpu.VMEM((pieces, QUARTER, D), jnp.bfloat16),
            pltpu.VMEM((SLOTS, D), jnp.bfloat16),
            pltpu.VMEM((pieces, SLOTS, QUARTER), jnp.bfloat16),
            pltpu.SemaphoreType.DMA((3 * pieces,)),
        ],
        compiler_params=pltpu.CompilerParams(vmem_limit_bytes=VMEM_LIMIT),
        name="expert_half",
    )(rows, *weights)


def combine_and_dispatch(terms, residual, attended, drift_in, gain, ids, gates):
    def body(terms_ref, residual_ref, attended_ref, drift_in_ref, gain_ref, ids_ref, gates_ref,
             result_ref, next_ref, send_ref, spread, packed, counts):
        moe = combine(terms_ref, ids_ref, gates_ref, 0, counts, spread)
        result = (residual_ref[...] + moe).astype(jnp.bfloat16)
        result_ref[...] = result
        inputs = jnp.concatenate(
            [result.astype(jnp.float32)[:BLOCK], drift_in_ref[1, 0].astype(jnp.float32)], axis=0
        )
        following = inputs + attended_ref[...]
        next_ref[...] = following
        dispatch(normalize(following, gain_ref[...]), ids_ref, 1, counts, spread, packed, send_ref)

    vmem = pl.BlockSpec(memory_space=pltpu.VMEM)
    return pl.pallas_call(
        body,
        in_specs=[vmem] * 5 + [smem_spec()] * 2,
        out_specs=[vmem] * 3,
        out_shape=[
            jax.ShapeDtypeStruct((ROWS, D), jnp.bfloat16),
            jax.ShapeDtypeStruct((ROWS, D), jnp.float32),
            jax.ShapeDtypeStruct((SLOTS, H, HD), jnp.bfloat16),
        ],
        scratch_shapes=[
            pltpu.VMEM((ROWS * H, HD), jnp.float32),
            pltpu.VMEM((ROWS, H, HD), jnp.bfloat16),
            pltpu.SMEM((EXPERTS,), jnp.int32),
        ],
        compiler_params=pltpu.CompilerParams(vmem_limit_bytes=VMEM_LIMIT),
        name="combine_and_dispatch",
    )(terms, residual, attended, drift_in, gain, ids, gates)


def combine_last(terms, residual, first_result, ids, gates):
    def body(terms_ref, residual_ref, first_ref, ids_ref, gates_ref, out_ref, spread, counts):
        moe = combine(terms_ref, ids_ref, gates_ref, 1, counts, spread)
        out_ref[0, 0] = first_ref[...]
        out_ref[1, 0] = (residual_ref[...] + moe).astype(jnp.bfloat16)

    vmem = pl.BlockSpec(memory_space=pltpu.VMEM)
    return pl.pallas_call(
        body,
        in_specs=[vmem] * 3 + [smem_spec()] * 2,
        out_specs=vmem,
        out_shape=jax.ShapeDtypeStruct((2, 1, ROWS, D), jnp.bfloat16),
        scratch_shapes=[
            pltpu.VMEM((ROWS * H, HD), jnp.float32),
            pltpu.SMEM((EXPERTS,), jnp.int32),
        ],
        compiler_params=pltpu.CompilerParams(vmem_limit_bytes=VMEM_LIMIT),
        name="combine_last",
    )(terms, residual, first_result, ids, gates)


def pairings(reps, exps):
    across, beside = [], []
    for r in range(reps):
        for e in range(exps):
            near, far = r ^ 1, reps - 1 - r
            if e % 2:
                near, far = far, near
            beside.append((r * exps + e, near * exps + e))
            across.append((r * exps + e, far * exps + e))
    return beside, across


def on_device(
    cache_keys,
    cache_values,
    lengths,
    drift_rows,
    block_in,
    drift_in,
    queries,
    new_keys,
    new_values,
    norm_gain,
    expert_ids,
    gate_weights,
    w_gate,
    w_up,
    w_down,
):
    axes = ("rep", "exp")
    beside, across = pairings(lax.axis_size("rep"), lax.axis_size("exp"))
    own = (w_gate[0], w_up[0], w_down[0])
    paired_gate = lax.ppermute(own[0], axes, beside)
    paired_gate, later = lax.optimization_barrier((paired_gate, own[1:]))
    paired = (paired_gate,) + tuple(lax.ppermute(part, axes, beside) for part in later)
    gain = norm_gain.reshape(1, D)
    gates = gate_weights.astype(jnp.float32)

    residual, send = first_attention(
        lengths, drift_rows, queries, cache_keys, cache_values, new_keys, new_values,
        block_in, drift_in, gain, expert_ids,
    )
    attended = second_attention(
        lengths, drift_rows, queries, cache_keys, cache_values, new_keys, new_values
    )

    def experts(send):
        rows = lax.all_to_all(send, "exp", split_axis=0, concat_axis=0, tiled=True)
        rows, weights = lax.optimization_barrier((rows, own + paired))
        visiting = lax.ppermute(rows, axes, across)
        home_terms = expert_half(rows, weights)
        away_terms = lax.ppermute(expert_half(visiting, weights), axes, across)
        terms = (home_terms.astype(jnp.float32) + away_terms.astype(jnp.float32)).astype(jnp.bfloat16)
        return lax.all_to_all(terms, "exp", split_axis=0, concat_axis=0, tiled=True)

    terms = experts(send)
    result, residual, send = combine_and_dispatch(
        terms, residual, attended, drift_in, gain, expert_ids, gates
    )
    terms = experts(send)
    return combine_last(terms, residual, result, expert_ids, gates)


def solution(mesh):
    placed = (
        P(("rep", "exp"), None, None),
        P(("rep", "exp"), None, None),
        P(("rep", "exp")),
        P(None, ("rep", "exp"), None),
        P(("rep", "exp"), None, None),
        P(None, ("rep", "exp"), None, None),
        P(None, ("rep", "exp"), None, None),
        P(None, ("rep", "exp"), None, None),
        P(None, ("rep", "exp"), None, None),
        P(),
        P(None, ("rep", "exp"), None, None),
        P(None, ("rep", "exp"), None, None),
        P("exp", None, "rep"),
        P("exp", None, "rep"),
        P("exp", "rep", None),
    )
    return jax.shard_map(
        on_device,
        mesh=mesh,
        in_specs=placed,
        out_specs=P(None, ("rep", "exp"), None, None),
        check_vma=False,
    )
```

```python
import jax
import jax.numpy as jnp
from jax import lax
from jax.experimental import pallas as pl
from jax.experimental.pallas import tpu as pltpu
from jax.sharding import PartitionSpec as P

H = 32
KVH = 4
GROUP = H // KVH
HD = 128
D = H * HD
TOP = 8
BLOCK = 8
ROWS = 16
CAP = 3
EXPERTS = 64
SLOTS = EXPERTS * CAP
CACHE = 2048
QUARTER = 256
NEG = -1e30
VMEM_LIMIT = 56 * 1024 * 1024


def smem_spec():
    return pl.BlockSpec(memory_space=pltpu.SMEM)


def each_slot(ids_ref, denoise, counts, visit):
    for e in range(EXPERTS):
        counts[e] = 0

    @pl.loop(0, ROWS)
    def _(t):
        picked = []
        for j in range(TOP):
            e = ids_ref[denoise, 0, t, j]
            c = counts[e]
            counts[e] = c + 1
            picked.append(e * CAP + jnp.minimum(c, CAP - 1))
        visit(t, picked)


def normalize(residual, gain):
    inverse = lax.rsqrt(jnp.mean(residual * residual, axis=-1, keepdims=True) + 1e-06)
    return residual * inverse * gain


def dispatch(normed, ids_ref, denoise, counts, spread, packed, send_ref):
    for k in range(H):
        spread[pl.ds(k, ROWS, stride=H), :] = normed[:, k * HD : (k + 1) * HD]
    packed[...] = spread[...].reshape(ROWS, H, HD).astype(jnp.bfloat16)
    send_ref[...] = jnp.zeros_like(send_ref)

    def visit(t, picked):
        row = packed[t]
        for slot in picked:
            send_ref[slot] = row

    each_slot(ids_ref, denoise, counts, visit)


def combine(terms_ref, ids_ref, gates_ref, denoise, counts, spread):
    def visit(t, picked):
        total = jnp.zeros((H, HD), jnp.float32)
        for j, slot in enumerate(picked):
            total = total + gates_ref[denoise, 0, t, j] * terms_ref[slot].astype(jnp.float32)
        spread[pl.ds(pl.multiple_of(t * H, H), H), :] = total

    each_slot(ids_ref, denoise, counts, visit)
    return jnp.concatenate([spread[pl.ds(k, ROWS, stride=H), :] for k in range(H)], axis=1)


def attend_head(denoise, lengths_ref, drift_ref, q_ref, k_ref, v_ref, nk_ref, nv_ref, bias, attended):
    head = pl.program_id(0)
    extra = ROWS * (denoise + 1)

    @pl.when(head == 0)
    def _():
        place = lax.broadcasted_iota(jnp.int32, (1, CACHE), 1)
        admitted = place < lengths_ref[0]
        for step in range(denoise + 1):
            for b in range(BLOCK):
                admitted = admitted & (place != drift_ref[step, 0, b])
        bias[...] = jnp.where(admitted, 0.0, NEG)

    queries = jnp.concatenate([q_ref[:, g * HD : (g + 1) * HD] for g in range(GROUP)], axis=0)
    contract_last = (((1,), (1,)), ((), ()))
    scale = HD ** (-0.5)
    scores = lax.dot_general(queries, k_ref[...], contract_last, preferred_element_type=jnp.float32)
    scores = scores * scale + bias[...]
    fresh_k = nk_ref[0 : denoise + 1].reshape(extra, HD)
    fresh_v = nv_ref[0 : denoise + 1].reshape(extra, HD)
    fresh = lax.dot_general(queries, fresh_k, contract_last, preferred_element_type=jnp.float32)
    row = lax.broadcasted_iota(jnp.int32, (GROUP * ROWS, extra), 0)
    col = lax.broadcasted_iota(jnp.int32, (GROUP * ROWS, extra), 1)
    place = col % ROWS
    allowed = (col >= denoise * ROWS) & ((place >= BLOCK) | (row % ROWS < BLOCK))
    if denoise == 1:
        for b in range(BLOCK):
            kept = drift_ref[1, 0, 0] != drift_ref[0, 0, b]
            for other in range(1, BLOCK):
                kept = kept & (drift_ref[1, 0, other] != drift_ref[0, 0, b])
            allowed = allowed | ((col == BLOCK + b) & kept)
    fresh = jnp.where(allowed, fresh * scale, NEG)
    peak = jnp.maximum(
        jnp.max(scores, axis=-1, keepdims=True), jnp.max(fresh, axis=-1, keepdims=True)
    )
    scores = jnp.exp(scores - peak)
    fresh = jnp.exp(fresh - peak)
    denom = jnp.sum(scores, axis=-1, keepdims=True) + jnp.sum(fresh, axis=-1, keepdims=True)
    mixed = jnp.dot(scores.astype(jnp.bfloat16), v_ref[...], preferred_element_type=jnp.float32)
    mixed = mixed + jnp.dot(fresh.astype(jnp.bfloat16), fresh_v, preferred_element_type=jnp.float32)
    mixed = mixed / denom
    wide = jnp.concatenate([mixed[g * ROWS : (g + 1) * ROWS] for g in range(GROUP)], axis=1)
    attended[:, pl.ds(pl.multiple_of(head * GROUP * HD, GROUP * HD), GROUP * HD)] = wide


def attention_specs(denoise):
    return [
        smem_spec(),
        smem_spec(),
        pl.BlockSpec((None, None, ROWS, GROUP * HD), lambda h: (denoise, 0, 0, h)),
        pl.BlockSpec((None, CACHE, HD), lambda h: (0, 0, h)),
        pl.BlockSpec((None, CACHE, HD), lambda h: (0, 0, h)),
        pl.BlockSpec((2, None, ROWS, HD), lambda h: (0, 0, 0, h)),
        pl.BlockSpec((2, None, ROWS, HD), lambda h: (0, 0, 0, h)),
    ]


def first_attention(lengths, drift_rows, queries, keys, values, new_keys, new_values, block_in, drift_in, gain, ids):
    def body(lengths_ref, drift_ref, q_ref, k_ref, v_ref, nk_ref, nv_ref, block_ref, drift_in_ref, gain_ref, ids_ref,
             residual_ref, send_ref, bias, attended, spread, packed, counts):
        attend_head(0, lengths_ref, drift_ref, q_ref, k_ref, v_ref, nk_ref, nv_ref, bias, attended)

        @pl.when(pl.program_id(0) == KVH - 1)
        def _():
            inputs = jnp.concatenate(
                [block_ref[...].astype(jnp.float32), drift_in_ref[...].astype(jnp.float32)], axis=0
            )
            residual = inputs + attended[...]
            residual_ref[...] = residual
            dispatch(normalize(residual, gain_ref[...]), ids_ref, 0, counts, spread, packed, send_ref)

    return pl.pallas_call(
        body,
        grid=(KVH,),
        in_specs=attention_specs(0)
        + [
            pl.BlockSpec((None, BLOCK, D), lambda h: (0, 0, 0)),
            pl.BlockSpec((None, None, BLOCK, D), lambda h: (0, 0, 0, 0)),
            pl.BlockSpec((1, D), lambda h: (0, 0)),
            smem_spec(),
        ],
        out_specs=[
            pl.BlockSpec((ROWS, D), lambda h: (0, 0)),
            pl.BlockSpec((SLOTS, H, HD), lambda h: (0, 0, 0)),
        ],
        out_shape=[
            jax.ShapeDtypeStruct((ROWS, D), jnp.float32),
            jax.ShapeDtypeStruct((SLOTS, H, HD), jnp.bfloat16),
        ],
        scratch_shapes=[
            pltpu.VMEM((1, CACHE), jnp.float32),
            pltpu.VMEM((ROWS, D), jnp.float32),
            pltpu.VMEM((ROWS * H, HD), jnp.float32),
            pltpu.VMEM((ROWS, H, HD), jnp.bfloat16),
            pltpu.SMEM((EXPERTS,), jnp.int32),
        ],
        compiler_params=pltpu.CompilerParams(vmem_limit_bytes=VMEM_LIMIT),
        name="first_attention",
    )(lengths, drift_rows, queries, keys, values, new_keys, new_values, block_in, drift_in, gain, ids)


def second_attention(lengths, drift_rows, queries, keys, values, new_keys, new_values):
    def body(lengths_ref, drift_ref, q_ref, k_ref, v_ref, nk_ref, nv_ref, attended, bias):
        attend_head(1, lengths_ref, drift_ref, q_ref, k_ref, v_ref, nk_ref, nv_ref, bias, attended)

    return pl.pallas_call(
        body,
        grid=(KVH,),
        in_specs=attention_specs(1),
        out_specs=pl.BlockSpec((ROWS, D), lambda h: (0, 0)),
        out_shape=jax.ShapeDtypeStruct((ROWS, D), jnp.float32),
        scratch_shapes=[pltpu.VMEM((1, CACHE), jnp.float32)],
        compiler_params=pltpu.CompilerParams(vmem_limit_bytes=VMEM_LIMIT),
        name="second_attention",
    )(lengths, drift_rows, queries, keys, values, new_keys, new_values)


def expert_half(rows, weights):
    pieces, count = len(weights) // 3, rows.shape[0]

    def body(*refs):
        rows_ref = refs[0]
        weight_refs = refs[1 : 1 + 3 * pieces]
        out_ref = refs[1 + 3 * pieces]
        gate, up, down, flat, hidden, sems = refs[2 + 3 * pieces :]
        copies = []
        for p in range(pieces):
            for kind, target in enumerate((gate, up, down)):
                copies.append(
                    pltpu.make_async_copy(
                        weight_refs[3 * p + kind], target.at[p], sems.at[3 * p + kind]
                    )
                )
        for copy in copies:
            copy.start()
        for r in range(0, count, 16):
            wide = rows_ref[r : r + 16].astype(jnp.float32).reshape(16, D)
            flat[r : r + 16, :] = wide.astype(jnp.bfloat16)
        for p in range(pieces):
            copies[3 * p].wait()
            gated = jnp.dot(flat[...], gate[p], preferred_element_type=jnp.float32)
            copies[3 * p + 1].wait()
            raised = jnp.dot(flat[...], up[p], preferred_element_type=jnp.float32)
            hidden[p] = (jax.nn.silu(gated) * raised).astype(jnp.bfloat16)
        for p in range(pieces):
            copies[3 * p + 2].wait()
        width = 512
        for n in range(D // width):
            part = jnp.zeros((count, width), jnp.float32)
            for p in range(pieces):
                part = part + jnp.dot(
                    hidden[p], down[p, :, n * width : (n + 1) * width], preferred_element_type=jnp.float32
                )
            heads = width // HD
            out_ref[:, n * heads : (n + 1) * heads, :] = part.reshape(count, heads, HD).astype(jnp.bfloat16)

    return pl.pallas_call(
        body,
        in_specs=[pl.BlockSpec(memory_space=pltpu.VMEM)] + [pl.BlockSpec(memory_space=pl.ANY)] * (3 * pieces),
        out_specs=pl.BlockSpec(memory_space=pltpu.VMEM),
        out_shape=jax.ShapeDtypeStruct((count, H, HD), jnp.bfloat16),
        scratch_shapes=[
            pltpu.VMEM((pieces, D, QUARTER), jnp.bfloat16),
            pltpu.VMEM((pieces, D, QUARTER), jnp.bfloat16),
            pltpu.VMEM((pieces, QUARTER, D), jnp.bfloat16),
            pltpu.VMEM((count, D), jnp.bfloat16),
            pltpu.VMEM((pieces, count, QUARTER), jnp.bfloat16),
            pltpu.SemaphoreType.DMA((3 * pieces,)),
        ],
        compiler_params=pltpu.CompilerParams(vmem_limit_bytes=VMEM_LIMIT),
        name="expert_half",
    )(rows, *weights)


def add_halves(home, first, second):
    steps = 2
    size = SLOTS // (2 * steps)

    def body(home_ref, first_ref, second_ref, out_ref):
        def add(away_ref):
            total = home_ref[...].astype(jnp.float32) + away_ref[...].astype(jnp.float32)
            out_ref[...] = total.astype(jnp.bfloat16)

        pl.when(pl.program_id(0) < steps)(lambda: add(first_ref))
        pl.when(pl.program_id(0) >= steps)(lambda: add(second_ref))

    block = (size, H, HD)
    return pl.pallas_call(
        body,
        grid=(2 * steps,),
        in_specs=[
            pl.BlockSpec(block, lambda i: (i, 0, 0)),
            pl.BlockSpec(block, lambda i: (jnp.minimum(i, steps - 1), 0, 0)),
            pl.BlockSpec(block, lambda i: (jnp.maximum(i - steps, 0), 0, 0)),
        ],
        out_specs=pl.BlockSpec(block, lambda i: (i, 0, 0)),
        out_shape=jax.ShapeDtypeStruct((SLOTS, H, HD), jnp.bfloat16),
        name="add_halves",
    )(home, first, second)


def combine_and_dispatch(terms, residual, attended, drift_in, gain, ids, gates):
    def body(terms_ref, residual_ref, attended_ref, drift_in_ref, gain_ref, ids_ref, gates_ref,
             result_ref, next_ref, send_ref, spread, packed, counts):
        moe = combine(terms_ref, ids_ref, gates_ref, 0, counts, spread)
        result = (residual_ref[...] + moe).astype(jnp.bfloat16)
        result_ref[...] = result
        inputs = jnp.concatenate(
            [result.astype(jnp.float32)[:BLOCK], drift_in_ref[1, 0].astype(jnp.float32)], axis=0
        )
        following = inputs + attended_ref[...]
        next_ref[...] = following
        dispatch(normalize(following, gain_ref[...]), ids_ref, 1, counts, spread, packed, send_ref)

    vmem = pl.BlockSpec(memory_space=pltpu.VMEM)
    return pl.pallas_call(
        body,
        in_specs=[vmem] * 5 + [smem_spec()] * 2,
        out_specs=[vmem] * 3,
        out_shape=[
            jax.ShapeDtypeStruct((ROWS, D), jnp.bfloat16),
            jax.ShapeDtypeStruct((ROWS, D), jnp.float32),
            jax.ShapeDtypeStruct((SLOTS, H, HD), jnp.bfloat16),
        ],
        scratch_shapes=[
            pltpu.VMEM((ROWS * H, HD), jnp.float32),
            pltpu.VMEM((ROWS, H, HD), jnp.bfloat16),
            pltpu.SMEM((EXPERTS,), jnp.int32),
        ],
        compiler_params=pltpu.CompilerParams(vmem_limit_bytes=VMEM_LIMIT),
        name="combine_and_dispatch",
    )(terms, residual, attended, drift_in, gain, ids, gates)


def combine_last(terms, residual, first_result, ids, gates):
    def body(terms_ref, residual_ref, first_ref, ids_ref, gates_ref, out_ref, spread, counts):
        moe = combine(terms_ref, ids_ref, gates_ref, 1, counts, spread)
        out_ref[0, 0] = first_ref[...]
        out_ref[1, 0] = (residual_ref[...] + moe).astype(jnp.bfloat16)

    vmem = pl.BlockSpec(memory_space=pltpu.VMEM)
    return pl.pallas_call(
        body,
        in_specs=[vmem] * 3 + [smem_spec()] * 2,
        out_specs=vmem,
        out_shape=jax.ShapeDtypeStruct((2, 1, ROWS, D), jnp.bfloat16),
        scratch_shapes=[
            pltpu.VMEM((ROWS * H, HD), jnp.float32),
            pltpu.SMEM((EXPERTS,), jnp.int32),
        ],
        compiler_params=pltpu.CompilerParams(vmem_limit_bytes=VMEM_LIMIT),
        name="combine_last",
    )(terms, residual, first_result, ids, gates)


def pairings(reps, exps):
    across, beside = [], []
    for r in range(reps):
        for e in range(exps):
            near, far = r ^ 1, reps - 1 - r
            if e % 2:
                near, far = far, near
            beside.append((r * exps + e, near * exps + e))
            across.append((r * exps + e, far * exps + e))
    return beside, across


def on_device(
    cache_keys,
    cache_values,
    lengths,
    drift_rows,
    block_in,
    drift_in,
    queries,
    new_keys,
    new_values,
    norm_gain,
    expert_ids,
    gate_weights,
    w_gate,
    w_up,
    w_down,
):
    axes = ("rep", "exp")
    beside, across = pairings(lax.axis_size("rep"), lax.axis_size("exp"))
    own = (w_gate[0], w_up[0], w_down[0])
    paired_gate = lax.ppermute(own[0], axes, beside)
    paired_gate, later = lax.optimization_barrier((paired_gate, own[1:]))
    paired = (paired_gate,) + tuple(lax.ppermute(part, axes, beside) for part in later)
    gain = norm_gain.reshape(1, D)
    gates = gate_weights.astype(jnp.float32)

    residual, send = first_attention(
        lengths, drift_rows, queries, cache_keys, cache_values, new_keys, new_values,
        block_in, drift_in, gain, expert_ids,
    )
    attended = second_attention(
        lengths, drift_rows, queries, cache_keys, cache_values, new_keys, new_values
    )

    def experts(send):
        rows = lax.all_to_all(send, "exp", split_axis=0, concat_axis=0, tiled=True)
        rows, weights = lax.optimization_barrier((rows, own + paired))
        halves = [slice(0, SLOTS // 2), slice(SLOTS // 2, SLOTS)]
        visiting = [lax.ppermute(rows[half], axes, across) for half in halves]
        away_terms = [lax.ppermute(expert_half(part, weights), axes, across) for part in visiting]
        home_terms = expert_half(rows, weights)
        terms = add_halves(home_terms, *away_terms)
        return lax.all_to_all(terms, "exp", split_axis=0, concat_axis=0, tiled=True)

    terms = experts(send)
    result, residual, send = combine_and_dispatch(
        terms, residual, attended, drift_in, gain, expert_ids, gates
    )
    terms = experts(send)
    return combine_last(terms, residual, result, expert_ids, gates)


def solution(mesh):
    placed = (
        P(("rep", "exp"), None, None),
        P(("rep", "exp"), None, None),
        P(("rep", "exp")),
        P(None, ("rep", "exp"), None),
        P(("rep", "exp"), None, None),
        P(None, ("rep", "exp"), None, None),
        P(None, ("rep", "exp"), None, None),
        P(None, ("rep", "exp"), None, None),
        P(None, ("rep", "exp"), None, None),
        P(),
        P(None, ("rep", "exp"), None, None),
        P(None, ("rep", "exp"), None, None),
        P("exp", None, "rep"),
        P("exp", None, "rep"),
        P("exp", "rep", None),
    )
    return jax.shard_map(
        on_device,
        mesh=mesh,
        in_specs=placed,
        out_specs=P(None, ("rep", "exp"), None, None),
        check_vma=False,
    )
```

```python
import jax
import jax.numpy as jnp
from jax import lax
from jax.experimental import pallas as pl
from jax.experimental.pallas import tpu as pltpu
from jax.sharding import PartitionSpec as P

H = 32
KVH = 4
GROUP = H // KVH
HD = 128
D = H * HD
TOP = 8
BLOCK = 8
ROWS = 16
CAP = 3
EXPERTS = 64
SLOTS = EXPERTS * CAP
CACHE = 2048
QUARTER = 256
VISITS = 2
NEG = -1e30
VMEM_LIMIT = 24 * 1024 * 1024


def smem_spec():
    return pl.BlockSpec(memory_space=pltpu.SMEM)


def each_slot(ids_ref, denoise, counts, visit):
    for e in range(EXPERTS):
        counts[e] = 0

    @pl.loop(0, ROWS)
    def _(t):
        picked = []
        for j in range(TOP):
            e = ids_ref[denoise, 0, j, t]
            c = counts[e]
            counts[e] = c + 1
            picked.append(e * CAP + jnp.minimum(c, CAP - 1))
        visit(t, picked)


def normalize(residual, gain):
    inverse = lax.rsqrt(jnp.mean(residual * residual, axis=-1, keepdims=True) + 1e-06)
    return residual * inverse * gain


def dispatch(normed, ids_ref, denoise, counts, spread, packed, send_ref):
    for k in range(H):
        spread[pl.ds(k, ROWS, stride=H), :] = normed[:, k * HD : (k + 1) * HD]
    packed[...] = spread[...].reshape(ROWS, H, HD).astype(jnp.bfloat16)
    send_ref[...] = jnp.zeros_like(send_ref)

    def visit(t, picked):
        row = packed[t]
        for slot in picked:
            send_ref[slot] = row

    each_slot(ids_ref, denoise, counts, visit)


def combine(terms_ref, ids_ref, gates_ref, denoise, counts, spread):
    def visit(t, picked):
        total = jnp.zeros((H, HD), jnp.float32)
        for j, slot in enumerate(picked):
            total = total + gates_ref[denoise, 0, j, t] * terms_ref[slot].astype(jnp.float32)
        spread[pl.ds(pl.multiple_of(t * H, H), H), :] = total

    each_slot(ids_ref, denoise, counts, visit)
    return jnp.concatenate([spread[pl.ds(k, ROWS, stride=H), :] for k in range(H)], axis=1)


def attend_head(denoise, lengths_ref, drift_ref, q_ref, k_ref, v_ref, nk_ref, nv_ref, bias, attended):
    head = pl.program_id(0)
    extra = ROWS * (denoise + 1)

    @pl.when(head == 0)
    def _():
        place = lax.broadcasted_iota(jnp.int32, (1, CACHE), 1)
        admitted = place < lengths_ref[0]
        for step in range(denoise + 1):
            for b in range(BLOCK):
                admitted = admitted & (place != drift_ref[step, 0, b])
        bias[...] = jnp.where(admitted, 0.0, NEG)

    queries = jnp.concatenate([q_ref[:, g * HD : (g + 1) * HD] for g in range(GROUP)], axis=0)
    contract_last = (((1,), (1,)), ((), ()))
    scale = HD ** (-0.5)
    scores = lax.dot_general(queries, k_ref[...], contract_last, preferred_element_type=jnp.float32)
    scores = scores * scale + bias[...]
    fresh_k = nk_ref[0 : denoise + 1].reshape(extra, HD)
    fresh_v = nv_ref[0 : denoise + 1].reshape(extra, HD)
    fresh = lax.dot_general(queries, fresh_k, contract_last, preferred_element_type=jnp.float32)
    row = lax.broadcasted_iota(jnp.int32, (GROUP * ROWS, extra), 0)
    col = lax.broadcasted_iota(jnp.int32, (GROUP * ROWS, extra), 1)
    place = col % ROWS
    allowed = (col >= denoise * ROWS) & ((place >= BLOCK) | (row % ROWS < BLOCK))
    if denoise == 1:
        for b in range(BLOCK):
            kept = drift_ref[1, 0, 0] != drift_ref[0, 0, b]
            for other in range(1, BLOCK):
                kept = kept & (drift_ref[1, 0, other] != drift_ref[0, 0, b])
            allowed = allowed | ((col == BLOCK + b) & kept)
    fresh = jnp.where(allowed, fresh * scale, NEG)
    peak = jnp.maximum(
        jnp.max(scores, axis=-1, keepdims=True), jnp.max(fresh, axis=-1, keepdims=True)
    )
    scores = jnp.exp(scores - peak)
    fresh = jnp.exp(fresh - peak)
    denom = jnp.sum(scores, axis=-1, keepdims=True) + jnp.sum(fresh, axis=-1, keepdims=True)
    mixed = jnp.dot(scores.astype(jnp.bfloat16), v_ref[...], preferred_element_type=jnp.float32)
    mixed = mixed + jnp.dot(fresh.astype(jnp.bfloat16), fresh_v, preferred_element_type=jnp.float32)
    mixed = mixed / denom
    wide = jnp.concatenate([mixed[g * ROWS : (g + 1) * ROWS] for g in range(GROUP)], axis=1)
    attended[:, pl.ds(pl.multiple_of(head * GROUP * HD, GROUP * HD), GROUP * HD)] = wide


def attention_specs(denoise):
    return [
        smem_spec(),
        smem_spec(),
        pl.BlockSpec((None, None, ROWS, GROUP * HD), lambda h: (denoise, 0, 0, h)),
        pl.BlockSpec((None, CACHE, HD), lambda h: (0, 0, h)),
        pl.BlockSpec((None, CACHE, HD), lambda h: (0, 0, h)),
        pl.BlockSpec((2, None, ROWS, HD), lambda h: (0, 0, 0, h)),
        pl.BlockSpec((2, None, ROWS, HD), lambda h: (0, 0, 0, h)),
    ]


def first_attention(lengths, drift_rows, queries, keys, values, new_keys, new_values, block_in, drift_in, gain, ids):
    def body(lengths_ref, drift_ref, q_ref, k_ref, v_ref, nk_ref, nv_ref, block_ref, drift_in_ref, gain_ref, ids_ref,
             residual_ref, send_ref, bias, attended, spread, packed, counts):
        attend_head(0, lengths_ref, drift_ref, q_ref, k_ref, v_ref, nk_ref, nv_ref, bias, attended)

        @pl.when(pl.program_id(0) == KVH - 1)
        def _():
            inputs = jnp.concatenate(
                [block_ref[...].astype(jnp.float32), drift_in_ref[...].astype(jnp.float32)], axis=0
            )
            residual = inputs + attended[...]
            residual_ref[...] = residual
            dispatch(normalize(residual, gain_ref[...]), ids_ref, 0, counts, spread, packed, send_ref)

    return pl.pallas_call(
        body,
        grid=(KVH,),
        in_specs=attention_specs(0)
        + [
            pl.BlockSpec((None, BLOCK, D), lambda h: (0, 0, 0)),
            pl.BlockSpec((None, None, BLOCK, D), lambda h: (0, 0, 0, 0)),
            pl.BlockSpec((1, D), lambda h: (0, 0)),
            smem_spec(),
        ],
        out_specs=[
            pl.BlockSpec((ROWS, D), lambda h: (0, 0)),
            pl.BlockSpec((SLOTS, H, HD), lambda h: (0, 0, 0)),
        ],
        out_shape=[
            jax.ShapeDtypeStruct((ROWS, D), jnp.float32),
            jax.ShapeDtypeStruct((SLOTS, H, HD), jnp.bfloat16),
        ],
        scratch_shapes=[
            pltpu.VMEM((1, CACHE), jnp.float32),
            pltpu.VMEM((ROWS, D), jnp.float32),
            pltpu.VMEM((ROWS * H, HD), jnp.float32),
            pltpu.VMEM((ROWS, H, HD), jnp.bfloat16),
            pltpu.SMEM((EXPERTS,), jnp.int32),
        ],
        compiler_params=pltpu.CompilerParams(vmem_limit_bytes=56 * 1024 * 1024),
        name="first_attention",
    )(lengths, drift_rows, queries, keys, values, new_keys, new_values, block_in, drift_in, gain, ids)


def second_attention(lengths, drift_rows, queries, keys, values, new_keys, new_values):
    def body(lengths_ref, drift_ref, q_ref, k_ref, v_ref, nk_ref, nv_ref, attended, bias):
        attend_head(1, lengths_ref, drift_ref, q_ref, k_ref, v_ref, nk_ref, nv_ref, bias, attended)

    return pl.pallas_call(
        body,
        grid=(KVH,),
        in_specs=attention_specs(1),
        out_specs=pl.BlockSpec((ROWS, D), lambda h: (0, 0)),
        out_shape=jax.ShapeDtypeStruct((ROWS, D), jnp.float32),
        scratch_shapes=[pltpu.VMEM((1, CACHE), jnp.float32)],
        compiler_params=pltpu.CompilerParams(vmem_limit_bytes=VMEM_LIMIT),
        name="second_attention",
    )(lengths, drift_rows, queries, keys, values, new_keys, new_values)


def keep_in_vmem(weights):
    def body(*refs):
        sources, targets, sems = refs[: len(weights)], refs[len(weights) : -1], refs[-1]
        copies = [
            pltpu.make_async_copy(source, target, sems.at[i])
            for i, (source, target) in enumerate(zip(sources, targets))
        ]
        for copy in copies:
            copy.start()
        for copy in copies:
            copy.wait()

    return pl.pallas_call(
        body,
        in_specs=[pl.BlockSpec(memory_space=pl.ANY)] * len(weights),
        out_specs=[pl.BlockSpec(memory_space=pltpu.VMEM)] * len(weights),
        out_shape=[pltpu.VMEM(part.shape, part.dtype) for part in weights],
        scratch_shapes=[pltpu.SemaphoreType.DMA((len(weights),))],
        compiler_params=pltpu.CompilerParams(vmem_limit_bytes=VMEM_LIMIT),
        name="keep_in_vmem",
    )(*weights)


def expert_half(rows, weights):
    pieces, count = len(weights), rows.shape[0]

    def body(*refs):
        rows_ref, weight_refs = refs[0], refs[1 : 1 + 3 * pieces]
        out_ref, flat, hidden = refs[1 + 3 * pieces :]
        for r in range(0, count, 16):
            wide = rows_ref[r : r + 16].astype(jnp.float32).reshape(16, D)
            flat[r : r + 16, :] = wide.astype(jnp.bfloat16)
        for p in range(pieces):
            gated = jnp.dot(flat[...], weight_refs[3 * p][...], preferred_element_type=jnp.float32)
            raised = jnp.dot(flat[...], weight_refs[3 * p + 1][...], preferred_element_type=jnp.float32)
            hidden[p] = (jax.nn.silu(gated) * raised).astype(jnp.bfloat16)
        width = 512
        heads = width // HD
        for n in range(D // width):
            part = jnp.zeros((count, width), jnp.float32)
            for p in range(pieces):
                part = part + jnp.dot(
                    hidden[p],
                    weight_refs[3 * p + 2][:, n * width : (n + 1) * width],
                    preferred_element_type=jnp.float32,
                )
            out_ref[:, n * heads : (n + 1) * heads, :] = part.reshape(count, heads, HD).astype(jnp.bfloat16)

    vmem = pl.BlockSpec(memory_space=pltpu.VMEM)
    return pl.pallas_call(
        body,
        in_specs=[vmem] * (1 + 3 * pieces),
        out_specs=vmem,
        out_shape=jax.ShapeDtypeStruct((count, H, HD), jnp.bfloat16),
        scratch_shapes=[
            pltpu.VMEM((count, D), jnp.bfloat16),
            pltpu.VMEM((pieces, count, QUARTER), jnp.bfloat16),
        ],
        compiler_params=pltpu.CompilerParams(vmem_limit_bytes=VMEM_LIMIT),
        name="expert_half",
    )(rows, *[part for piece in weights for part in piece])


def add_part(terms, away, part):
    steps = 2
    size = away.shape[0] // steps
    block = (size, H, HD)

    def body(terms_ref, away_ref, out_ref):
        total = terms_ref[...].astype(jnp.float32) + away_ref[...].astype(jnp.float32)
        out_ref[...] = total.astype(jnp.bfloat16)

    return pl.pallas_call(
        body,
        grid=(steps,),
        in_specs=[
            pl.BlockSpec(block, lambda i: (part * steps + i, 0, 0)),
            pl.BlockSpec(block, lambda i: (i, 0, 0)),
        ],
        out_specs=pl.BlockSpec(block, lambda i: (part * steps + i, 0, 0)),
        out_shape=jax.ShapeDtypeStruct(terms.shape, terms.dtype),
        input_output_aliases={0: 0},
        compiler_params=pltpu.CompilerParams(vmem_limit_bytes=VMEM_LIMIT),
        name="add_part",
    )(terms, away)


def combine_and_dispatch(terms, residual, attended, drift_in, gain, ids, gates):
    def body(terms_ref, residual_ref, attended_ref, drift_in_ref, gain_ref, ids_ref, gates_ref,
             result_ref, next_ref, send_ref, spread, packed, counts):
        moe = combine(terms_ref, ids_ref, gates_ref, 0, counts, spread)
        result = (residual_ref[...] + moe).astype(jnp.bfloat16)
        result_ref[...] = result
        inputs = jnp.concatenate(
            [result.astype(jnp.float32)[:BLOCK], drift_in_ref[1, 0].astype(jnp.float32)], axis=0
        )
        following = inputs + attended_ref[...]
        next_ref[...] = following
        dispatch(normalize(following, gain_ref[...]), ids_ref, 1, counts, spread, packed, send_ref)

    vmem = pl.BlockSpec(memory_space=pltpu.VMEM)
    return pl.pallas_call(
        body,
        in_specs=[vmem] * 5 + [smem_spec()] * 2,
        out_specs=[vmem] * 3,
        out_shape=[
            jax.ShapeDtypeStruct((ROWS, D), jnp.bfloat16),
            jax.ShapeDtypeStruct((ROWS, D), jnp.float32),
            jax.ShapeDtypeStruct((SLOTS, H, HD), jnp.bfloat16),
        ],
        scratch_shapes=[
            pltpu.VMEM((ROWS * H, HD), jnp.float32),
            pltpu.VMEM((ROWS, H, HD), jnp.bfloat16),
            pltpu.SMEM((EXPERTS,), jnp.int32),
        ],
        compiler_params=pltpu.CompilerParams(vmem_limit_bytes=VMEM_LIMIT),
        name="combine_and_dispatch",
    )(terms, residual, attended, drift_in, gain, ids, gates)


def combine_last(terms, residual, first_result, ids, gates):
    def body(terms_ref, residual_ref, first_ref, ids_ref, gates_ref, out_ref, spread, counts):
        moe = combine(terms_ref, ids_ref, gates_ref, 1, counts, spread)
        out_ref[0, 0] = first_ref[...]
        out_ref[1, 0] = (residual_ref[...] + moe).astype(jnp.bfloat16)

    vmem = pl.BlockSpec(memory_space=pltpu.VMEM)
    return pl.pallas_call(
        body,
        in_specs=[vmem] * 3 + [smem_spec()] * 2,
        out_specs=vmem,
        out_shape=jax.ShapeDtypeStruct((2, 1, ROWS, D), jnp.bfloat16),
        scratch_shapes=[
            pltpu.VMEM((ROWS * H, HD), jnp.float32),
            pltpu.SMEM((EXPERTS,), jnp.int32),
        ],
        compiler_params=pltpu.CompilerParams(vmem_limit_bytes=VMEM_LIMIT),
        name="combine_last",
    )(terms, residual, first_result, ids, gates)


def pairings(reps, exps):
    across, beside = [], []
    for r in range(reps):
        for e in range(exps):
            near, far = r ^ 1, reps - 1 - r
            if e % 2:
                near, far = far, near
            beside.append((r * exps + e, near * exps + e))
            across.append((r * exps + e, far * exps + e))
    return beside, across


def on_device(
    cache_keys,
    cache_values,
    lengths,
    drift_rows,
    block_in,
    drift_in,
    queries,
    new_keys,
    new_values,
    norm_gain,
    expert_ids,
    gate_weights,
    w_gate,
    w_up,
    w_down,
):
    axes = ("rep", "exp")
    beside, across = pairings(lax.axis_size("rep"), lax.axis_size("exp"))
    own = (w_gate[0], w_up[0], w_down[0])
    paired_gate = lax.ppermute(own[0], axes, beside)
    paired_gate, later = lax.optimization_barrier((paired_gate, own[1:]))
    paired = (paired_gate,) + tuple(lax.ppermute(part, axes, beside) for part in later)
    gain = norm_gain.reshape(1, D)
    expert_ids = jnp.swapaxes(expert_ids, 2, 3)
    gates = jnp.swapaxes(gate_weights, 2, 3).astype(jnp.float32)

    residual, send = first_attention(
        lengths, drift_rows, queries, cache_keys, cache_values, new_keys, new_values,
        block_in, drift_in, gain, expert_ids,
    )
    attended = second_attention(
        lengths, drift_rows, queries, cache_keys, cache_values, new_keys, new_values
    )

    weights = (keep_in_vmem(own), keep_in_vmem(paired))

    def experts(send):
        rows = lax.all_to_all(send, "exp", split_axis=0, concat_axis=0, tiled=True)
        rows, _ = lax.optimization_barrier((rows, paired))
        size = SLOTS // VISITS
        visiting = [lax.ppermute(rows[i * size : (i + 1) * size], axes, across) for i in range(VISITS)]
        away_terms = [lax.ppermute(expert_half(part, weights), axes, across) for part in visiting]
        terms = expert_half(rows, weights)
        for i, away in enumerate(away_terms):
            terms = add_part(terms, away, i)
        return lax.all_to_all(terms, "exp", split_axis=0, concat_axis=0, tiled=True)

    terms = experts(send)
    result, residual, send = combine_and_dispatch(
        terms, residual, attended, drift_in, gain, expert_ids, gates
    )
    terms = experts(send)
    return combine_last(terms, residual, result, expert_ids, gates)


def solution(mesh):
    placed = (
        P(("rep", "exp"), None, None),
        P(("rep", "exp"), None, None),
        P(("rep", "exp")),
        P(None, ("rep", "exp"), None),
        P(("rep", "exp"), None, None),
        P(None, ("rep", "exp"), None, None),
        P(None, ("rep", "exp"), None, None),
        P(None, ("rep", "exp"), None, None),
        P(None, ("rep", "exp"), None, None),
        P(),
        P(None, ("rep", "exp"), None, None),
        P(None, ("rep", "exp"), None, None),
        P("exp", None, "rep"),
        P("exp", None, "rep"),
        P("exp", "rep", None),
    )
    return jax.shard_map(
        on_device,
        mesh=mesh,
        in_specs=placed,
        out_specs=P(None, ("rep", "exp"), None, None),
        check_vma=False,
    )
```

```python
import jax
import jax.numpy as jnp
from jax import lax
from jax.experimental import pallas as pl
from jax.experimental.pallas import tpu as pltpu
from jax.sharding import PartitionSpec as P

H = 32
KVH = 4
GROUP = H // KVH
HD = 128
D = H * HD
TOP = 8
BLOCK = 8
ROWS = 16
CAP = 3
EXPERTS = 64
SLOTS = EXPERTS * CAP
CACHE = 2048
QUARTER = 256
VISITS = 2
NEG = -1e30
VMEM_LIMIT = 24 * 1024 * 1024


def smem_spec():
    return pl.BlockSpec(memory_space=pltpu.SMEM)


def each_slot(ids_ref, denoise, counts, visit):
    for e in range(EXPERTS):
        counts[e] = 0

    @pl.loop(0, ROWS)
    def _(t):
        picked = []
        for j in range(TOP):
            e = ids_ref[denoise, 0, j, t]
            c = counts[e]
            counts[e] = c + 1
            picked.append(e * CAP + jnp.minimum(c, CAP - 1))
        visit(t, picked)


def normalize(residual, gain):
    inverse = lax.rsqrt(jnp.mean(residual * residual, axis=-1, keepdims=True) + 1e-06)
    return residual * inverse * gain


def dispatch(normed, ids_ref, denoise, counts, spread, packed, send_ref):
    for k in range(H):
        spread[pl.ds(k, ROWS, stride=H), :] = normed[:, k * HD : (k + 1) * HD]
    packed[...] = spread[...].reshape(ROWS, H, HD).astype(jnp.bfloat16)
    send_ref[...] = jnp.zeros_like(send_ref)

    def visit(t, picked):
        row = packed[t]
        for slot in picked:
            send_ref[slot] = row

    each_slot(ids_ref, denoise, counts, visit)


def combine(terms_ref, ids_ref, gates_ref, denoise, counts, spread):
    def visit(t, picked):
        total = jnp.zeros((H, HD), jnp.float32)
        for j, slot in enumerate(picked):
            total = total + gates_ref[denoise, 0, j, t] * terms_ref[slot].astype(jnp.float32)
        spread[pl.ds(pl.multiple_of(t * H, H), H), :] = total

    each_slot(ids_ref, denoise, counts, visit)
    return jnp.concatenate([spread[pl.ds(k, ROWS, stride=H), :] for k in range(H)], axis=1)


def attend_head(denoise, lengths_ref, drift_ref, q_ref, k_ref, v_ref, nk_ref, nv_ref, bias, attended):
    head = pl.program_id(0)
    extra = ROWS * (denoise + 1)

    @pl.when(head == 0)
    def _():
        place = lax.broadcasted_iota(jnp.int32, (1, CACHE), 1)
        admitted = place < lengths_ref[0]
        for step in range(denoise + 1):
            for b in range(BLOCK):
                admitted = admitted & (place != drift_ref[step, 0, b])
        bias[...] = jnp.where(admitted, 0.0, NEG)

    queries = jnp.concatenate([q_ref[:, g * HD : (g + 1) * HD] for g in range(GROUP)], axis=0)
    contract_last = (((1,), (1,)), ((), ()))
    scale = HD ** (-0.5)
    scores = lax.dot_general(queries, k_ref[...], contract_last, preferred_element_type=jnp.float32)
    scores = scores * scale + bias[...]
    fresh_k = nk_ref[0 : denoise + 1].reshape(extra, HD)
    fresh_v = nv_ref[0 : denoise + 1].reshape(extra, HD)
    fresh = lax.dot_general(queries, fresh_k, contract_last, preferred_element_type=jnp.float32)
    row = lax.broadcasted_iota(jnp.int32, (GROUP * ROWS, extra), 0)
    col = lax.broadcasted_iota(jnp.int32, (GROUP * ROWS, extra), 1)
    place = col % ROWS
    allowed = (col >= denoise * ROWS) & ((place >= BLOCK) | (row % ROWS < BLOCK))
    if denoise == 1:
        for b in range(BLOCK):
            kept = drift_ref[1, 0, 0] != drift_ref[0, 0, b]
            for other in range(1, BLOCK):
                kept = kept & (drift_ref[1, 0, other] != drift_ref[0, 0, b])
            allowed = allowed | ((col == BLOCK + b) & kept)
    fresh = jnp.where(allowed, fresh * scale, NEG)
    peak = jnp.maximum(
        jnp.max(scores, axis=-1, keepdims=True), jnp.max(fresh, axis=-1, keepdims=True)
    )
    scores = jnp.exp(scores - peak)
    fresh = jnp.exp(fresh - peak)
    denom = jnp.sum(scores, axis=-1, keepdims=True) + jnp.sum(fresh, axis=-1, keepdims=True)
    mixed = jnp.dot(scores.astype(jnp.bfloat16), v_ref[...], preferred_element_type=jnp.float32)
    mixed = mixed + jnp.dot(fresh.astype(jnp.bfloat16), fresh_v, preferred_element_type=jnp.float32)
    mixed = mixed / denom
    wide = jnp.concatenate([mixed[g * ROWS : (g + 1) * ROWS] for g in range(GROUP)], axis=1)
    attended[:, pl.ds(pl.multiple_of(head * GROUP * HD, GROUP * HD), GROUP * HD)] = wide


def attention_specs(denoise):
    return [
        smem_spec(),
        smem_spec(),
        pl.BlockSpec((None, None, ROWS, GROUP * HD), lambda h: (denoise, 0, 0, h)),
        pl.BlockSpec((None, CACHE, HD), lambda h: (0, 0, h)),
        pl.BlockSpec((None, CACHE, HD), lambda h: (0, 0, h)),
        pl.BlockSpec((2, None, ROWS, HD), lambda h: (0, 0, 0, h)),
        pl.BlockSpec((2, None, ROWS, HD), lambda h: (0, 0, 0, h)),
    ]


def first_attention(lengths, drift_rows, queries, keys, values, new_keys, new_values, block_in, drift_in, gain, ids):
    def body(lengths_ref, drift_ref, q_ref, k_ref, v_ref, nk_ref, nv_ref, block_ref, drift_in_ref, gain_ref, ids_ref,
             residual_ref, send_ref, bias, attended, spread, packed, counts):
        attend_head(0, lengths_ref, drift_ref, q_ref, k_ref, v_ref, nk_ref, nv_ref, bias, attended)

        @pl.when(pl.program_id(0) == KVH - 1)
        def _():
            inputs = jnp.concatenate(
                [block_ref[...].astype(jnp.float32), drift_in_ref[...].astype(jnp.float32)], axis=0
            )
            residual = inputs + attended[...]
            residual_ref[...] = residual
            dispatch(normalize(residual, gain_ref[...]), ids_ref, 0, counts, spread, packed, send_ref)

    return pl.pallas_call(
        body,
        grid=(KVH,),
        in_specs=attention_specs(0)
        + [
            pl.BlockSpec((None, BLOCK, D), lambda h: (0, 0, 0)),
            pl.BlockSpec((None, None, BLOCK, D), lambda h: (0, 0, 0, 0)),
            pl.BlockSpec((1, D), lambda h: (0, 0)),
            smem_spec(),
        ],
        out_specs=[
            pl.BlockSpec((ROWS, D), lambda h: (0, 0)),
            pl.BlockSpec((SLOTS, H, HD), lambda h: (0, 0, 0)),
        ],
        out_shape=[
            jax.ShapeDtypeStruct((ROWS, D), jnp.float32),
            jax.ShapeDtypeStruct((SLOTS, H, HD), jnp.bfloat16),
        ],
        scratch_shapes=[
            pltpu.VMEM((1, CACHE), jnp.float32),
            pltpu.VMEM((ROWS, D), jnp.float32),
            pltpu.VMEM((ROWS * H, HD), jnp.float32),
            pltpu.VMEM((ROWS, H, HD), jnp.bfloat16),
            pltpu.SMEM((EXPERTS,), jnp.int32),
        ],
        compiler_params=pltpu.CompilerParams(vmem_limit_bytes=56 * 1024 * 1024),
        name="first_attention",
    )(lengths, drift_rows, queries, keys, values, new_keys, new_values, block_in, drift_in, gain, ids)


def second_attention(lengths, drift_rows, queries, keys, values, new_keys, new_values):
    def body(lengths_ref, drift_ref, q_ref, k_ref, v_ref, nk_ref, nv_ref, attended, bias):
        attend_head(1, lengths_ref, drift_ref, q_ref, k_ref, v_ref, nk_ref, nv_ref, bias, attended)

    return pl.pallas_call(
        body,
        grid=(KVH,),
        in_specs=attention_specs(1),
        out_specs=pl.BlockSpec((ROWS, D), lambda h: (0, 0)),
        out_shape=jax.ShapeDtypeStruct((ROWS, D), jnp.float32),
        scratch_shapes=[pltpu.VMEM((1, CACHE), jnp.float32)],
        compiler_params=pltpu.CompilerParams(vmem_limit_bytes=VMEM_LIMIT),
        name="second_attention",
    )(lengths, drift_rows, queries, keys, values, new_keys, new_values)


def keep_in_vmem(weights):
    downs = weights[2:]
    shapes = (weights[0].shape, weights[1].shape, (sum(part.shape[0] for part in downs), D))

    def body(*refs):
        sources, (gate, up, down), sems = refs[: len(weights)], refs[len(weights) : -1], refs[-1]
        targets, row = [gate, up], 0
        for part in downs:
            targets.append(down.at[row : row + part.shape[0]])
            row += part.shape[0]
        copies = [
            pltpu.make_async_copy(source, target, sems.at[i])
            for i, (source, target) in enumerate(zip(sources, targets))
        ]
        for copy in copies:
            copy.start()
        for copy in copies:
            copy.wait()

    return pl.pallas_call(
        body,
        in_specs=[pl.BlockSpec(memory_space=pl.ANY)] * len(weights),
        out_specs=[pl.BlockSpec(memory_space=pltpu.VMEM)] * 3,
        out_shape=[pltpu.VMEM(shape, jnp.bfloat16) for shape in shapes],
        scratch_shapes=[pltpu.SemaphoreType.DMA((len(weights),))],
        compiler_params=pltpu.CompilerParams(vmem_limit_bytes=VMEM_LIMIT),
        name="keep_in_vmem",
    )(*weights)


def expert_half(rows, weights):
    pieces, count = len(weights), rows.shape[0]

    def body(*refs):
        rows_ref, weight_refs = refs[0], refs[1 : 1 + 3 * pieces]
        out_ref, flat, hidden = refs[1 + 3 * pieces :]
        for r in range(0, count, 16):
            wide = rows_ref[r : r + 16].astype(jnp.float32).reshape(16, D)
            flat[r : r + 16, :] = wide.astype(jnp.bfloat16)
        for p in range(pieces):
            gated = jnp.dot(flat[...], weight_refs[3 * p][...], preferred_element_type=jnp.float32)
            raised = jnp.dot(flat[...], weight_refs[3 * p + 1][...], preferred_element_type=jnp.float32)
            hidden[p] = (jax.nn.silu(gated) * raised).astype(jnp.bfloat16)
        width = 512
        heads = width // HD
        for n in range(D // width):
            part = jnp.zeros((count, width), jnp.float32)
            for p in range(pieces):
                part = part + jnp.dot(
                    hidden[p],
                    weight_refs[3 * p + 2][:, n * width : (n + 1) * width],
                    preferred_element_type=jnp.float32,
                )
            out_ref[:, n * heads : (n + 1) * heads, :] = part.reshape(count, heads, HD).astype(jnp.bfloat16)

    vmem = pl.BlockSpec(memory_space=pltpu.VMEM)
    return pl.pallas_call(
        body,
        in_specs=[vmem] * (1 + 3 * pieces),
        out_specs=vmem,
        out_shape=jax.ShapeDtypeStruct((count, H, HD), jnp.bfloat16),
        scratch_shapes=[
            pltpu.VMEM((count, D), jnp.bfloat16),
            pltpu.VMEM((pieces, count, QUARTER), jnp.bfloat16),
        ],
        compiler_params=pltpu.CompilerParams(vmem_limit_bytes=VMEM_LIMIT),
        name="expert_half",
    )(rows, *[part for piece in weights for part in piece])


def add_part(terms, away, part):
    steps = 2
    size = away.shape[0] // steps
    block = (size, H, HD)

    def body(terms_ref, away_ref, out_ref):
        total = terms_ref[...].astype(jnp.float32) + away_ref[...].astype(jnp.float32)
        out_ref[...] = total.astype(jnp.bfloat16)

    return pl.pallas_call(
        body,
        grid=(steps,),
        in_specs=[
            pl.BlockSpec(block, lambda i: (part * steps + i, 0, 0)),
            pl.BlockSpec(block, lambda i: (i, 0, 0)),
        ],
        out_specs=pl.BlockSpec(block, lambda i: (part * steps + i, 0, 0)),
        out_shape=jax.ShapeDtypeStruct(terms.shape, terms.dtype),
        input_output_aliases={0: 0},
        compiler_params=pltpu.CompilerParams(vmem_limit_bytes=VMEM_LIMIT),
        name="add_part",
    )(terms, away)


def combine_and_dispatch(terms, residual, attended, drift_in, gain, ids, gates):
    def body(terms_ref, residual_ref, attended_ref, drift_in_ref, gain_ref, ids_ref, gates_ref,
             result_ref, next_ref, send_ref, spread, packed, counts):
        moe = combine(terms_ref, ids_ref, gates_ref, 0, counts, spread)
        result = (residual_ref[...] + moe).astype(jnp.bfloat16)
        result_ref[...] = result
        inputs = jnp.concatenate(
            [result.astype(jnp.float32)[:BLOCK], drift_in_ref[1, 0].astype(jnp.float32)], axis=0
        )
        following = inputs + attended_ref[...]
        next_ref[...] = following
        dispatch(normalize(following, gain_ref[...]), ids_ref, 1, counts, spread, packed, send_ref)

    vmem = pl.BlockSpec(memory_space=pltpu.VMEM)
    return pl.pallas_call(
        body,
        in_specs=[vmem] * 5 + [smem_spec()] * 2,
        out_specs=[vmem] * 3,
        out_shape=[
            jax.ShapeDtypeStruct((ROWS, D), jnp.bfloat16),
            jax.ShapeDtypeStruct((ROWS, D), jnp.float32),
            jax.ShapeDtypeStruct((SLOTS, H, HD), jnp.bfloat16),
        ],
        scratch_shapes=[
            pltpu.VMEM((ROWS * H, HD), jnp.float32),
            pltpu.VMEM((ROWS, H, HD), jnp.bfloat16),
            pltpu.SMEM((EXPERTS,), jnp.int32),
        ],
        compiler_params=pltpu.CompilerParams(vmem_limit_bytes=VMEM_LIMIT),
        name="combine_and_dispatch",
    )(terms, residual, attended, drift_in, gain, ids, gates)


def combine_last(terms, residual, first_result, ids, gates):
    def body(terms_ref, residual_ref, first_ref, ids_ref, gates_ref, out_ref, spread, counts):
        moe = combine(terms_ref, ids_ref, gates_ref, 1, counts, spread)
        out_ref[0, 0] = first_ref[...]
        out_ref[1, 0] = (residual_ref[...] + moe).astype(jnp.bfloat16)

    vmem = pl.BlockSpec(memory_space=pltpu.VMEM)
    return pl.pallas_call(
        body,
        in_specs=[vmem] * 3 + [smem_spec()] * 2,
        out_specs=vmem,
        out_shape=jax.ShapeDtypeStruct((2, 1, ROWS, D), jnp.bfloat16),
        scratch_shapes=[
            pltpu.VMEM((ROWS * H, HD), jnp.float32),
            pltpu.SMEM((EXPERTS,), jnp.int32),
        ],
        compiler_params=pltpu.CompilerParams(vmem_limit_bytes=VMEM_LIMIT),
        name="combine_last",
    )(terms, residual, first_result, ids, gates)


def pairings(reps, exps):
    across, beside = [], []
    for r in range(reps):
        for e in range(exps):
            near, far = r ^ 1, reps - 1 - r
            if e % 2:
                near, far = far, near
            beside.append((r * exps + e, near * exps + e))
            across.append((r * exps + e, far * exps + e))
    return beside, across


def on_device(
    cache_keys,
    cache_values,
    lengths,
    drift_rows,
    block_in,
    drift_in,
    queries,
    new_keys,
    new_values,
    norm_gain,
    expert_ids,
    gate_weights,
    w_gate,
    w_up,
    w_down,
):
    axes = ("rep", "exp")
    beside, across = pairings(lax.axis_size("rep"), lax.axis_size("exp"))
    own = (w_gate[0], w_up[0], w_down[0])
    gate_up = [lax.ppermute(part, axes, beside) for part in own[:2]]
    downs = []
    for i, half in enumerate(jnp.split(own[2], 2)):
        gate_up[i], half = lax.optimization_barrier((gate_up[i], half))
        downs.append(lax.ppermute(half, axes, beside))
    paired = (*gate_up, *downs)
    gain = norm_gain.reshape(1, D)
    expert_ids = jnp.swapaxes(expert_ids, 2, 3)
    gates = jnp.swapaxes(gate_weights, 2, 3).astype(jnp.float32)

    residual, send = first_attention(
        lengths, drift_rows, queries, cache_keys, cache_values, new_keys, new_values,
        block_in, drift_in, gain, expert_ids,
    )
    attended = second_attention(
        lengths, drift_rows, queries, cache_keys, cache_values, new_keys, new_values
    )

    weights = (keep_in_vmem(own), keep_in_vmem(paired))

    def experts(send, first):
        rows = lax.all_to_all(send, "exp", split_axis=0, concat_axis=0, tiled=True)
        rows, first = lax.optimization_barrier((rows, first))
        size = SLOTS // VISITS
        visiting = [lax.ppermute(rows[i * size : (i + 1) * size], axes, across) for i in range(VISITS)]
        away_terms = [lax.ppermute(expert_half(part, weights), axes, across) for part in visiting]
        terms = expert_half(rows, weights)
        for i, away in enumerate(away_terms):
            terms = add_part(terms, away, i)
        return lax.all_to_all(terms, "exp", split_axis=0, concat_axis=0, tiled=True), first

    terms, (_, attended, gates) = experts(send, (paired, attended, gates))
    result, residual, send = combine_and_dispatch(
        terms, residual, attended, drift_in, gain, expert_ids, gates
    )
    terms, _ = experts(send, paired)
    return combine_last(terms, residual, result, expert_ids, gates)


def solution(mesh):
    placed = (
        P(("rep", "exp"), None, None),
        P(("rep", "exp"), None, None),
        P(("rep", "exp")),
        P(None, ("rep", "exp"), None),
        P(("rep", "exp"), None, None),
        P(None, ("rep", "exp"), None, None),
        P(None, ("rep", "exp"), None, None),
        P(None, ("rep", "exp"), None, None),
        P(None, ("rep", "exp"), None, None),
        P(),
        P(None, ("rep", "exp"), None, None),
        P(None, ("rep", "exp"), None, None),
        P("exp", None, "rep"),
        P("exp", None, "rep"),
        P("exp", "rep", None),
    )
    return jax.shard_map(
        on_device,
        mesh=mesh,
        in_specs=placed,
        out_specs=P(None, ("rep", "exp"), None, None),
        check_vma=False,
    )
```

```python
import jax
import jax.numpy as jnp
from jax import lax
from jax.experimental import pallas as pl
from jax.experimental.pallas import tpu as pltpu
from jax.sharding import PartitionSpec as P

H = 32
KVH = 4
GROUP = H // KVH
HD = 128
D = H * HD
TOP = 8
BLOCK = 8
ROWS = 16
CAP = 3
EXPERTS = 64
SLOTS = EXPERTS * CAP
CACHE = 2048
QUARTER = 256
VISITS = 2
NEG = -1e30
VMEM_LIMIT = 24 * 1024 * 1024


def smem_spec():
    return pl.BlockSpec(memory_space=pltpu.SMEM)


def each_slot(ids_ref, denoise, counts, visit):
    for e in range(EXPERTS):
        counts[e] = 0

    @pl.loop(0, ROWS)
    def _(t):
        picked = []
        for j in range(TOP):
            e = ids_ref[denoise, 0, j, t]
            c = counts[e]
            counts[e] = c + 1
            picked.append(e * CAP + jnp.minimum(c, CAP - 1))
        visit(t, picked)


def normalize(residual, gain):
    inverse = lax.rsqrt(jnp.mean(residual * residual, axis=-1, keepdims=True) + 1e-06)
    return residual * inverse * gain


def dispatch(normed, ids_ref, denoise, counts, spread, packed, send_ref):
    for k in range(H):
        spread[pl.ds(k, ROWS, stride=H), :] = normed[:, k * HD : (k + 1) * HD]
    packed[...] = spread[...].reshape(ROWS, H, HD).astype(jnp.bfloat16)
    send_ref[...] = jnp.zeros_like(send_ref)

    def visit(t, picked):
        row = packed[t]
        for slot in picked:
            send_ref[slot] = row

    each_slot(ids_ref, denoise, counts, visit)


def combine(terms_ref, ids_ref, gates_ref, denoise, counts, spread):
    def visit(t, picked):
        total = jnp.zeros((H, HD), jnp.float32)
        for j, slot in enumerate(picked):
            total = total + gates_ref[denoise, 0, j, t] * terms_ref[slot].astype(jnp.float32)
        spread[pl.ds(pl.multiple_of(t * H, H), H), :] = total

    each_slot(ids_ref, denoise, counts, visit)
    return jnp.concatenate([spread[pl.ds(k, ROWS, stride=H), :] for k in range(H)], axis=1)


def attend_head(denoise, lengths_ref, drift_ref, q_ref, k_ref, v_ref, nk_ref, nv_ref, bias, attended):
    head = pl.program_id(0)
    extra = ROWS * (denoise + 1)

    @pl.when(head == 0)
    def _():
        place = lax.broadcasted_iota(jnp.int32, (1, CACHE), 1)
        admitted = place < lengths_ref[0]
        for step in range(denoise + 1):
            for b in range(BLOCK):
                admitted = admitted & (place != drift_ref[step, 0, b])
        bias[...] = jnp.where(admitted, 0.0, NEG)

    queries = jnp.concatenate([q_ref[:, g * HD : (g + 1) * HD] for g in range(GROUP)], axis=0)
    contract_last = (((1,), (1,)), ((), ()))
    scale = HD ** (-0.5)
    scores = lax.dot_general(queries, k_ref[...], contract_last, preferred_element_type=jnp.float32)
    scores = scores * scale + bias[...]
    fresh_k = nk_ref[0 : denoise + 1].reshape(extra, HD)
    fresh_v = nv_ref[0 : denoise + 1].reshape(extra, HD)
    fresh = lax.dot_general(queries, fresh_k, contract_last, preferred_element_type=jnp.float32)
    row = lax.broadcasted_iota(jnp.int32, (GROUP * ROWS, extra), 0)
    col = lax.broadcasted_iota(jnp.int32, (GROUP * ROWS, extra), 1)
    place = col % ROWS
    allowed = (col >= denoise * ROWS) & ((place >= BLOCK) | (row % ROWS < BLOCK))
    if denoise == 1:
        for b in range(BLOCK):
            kept = drift_ref[1, 0, 0] != drift_ref[0, 0, b]
            for other in range(1, BLOCK):
                kept = kept & (drift_ref[1, 0, other] != drift_ref[0, 0, b])
            allowed = allowed | ((col == BLOCK + b) & kept)
    fresh = jnp.where(allowed, fresh * scale, NEG)
    peak = jnp.maximum(
        jnp.max(scores, axis=-1, keepdims=True), jnp.max(fresh, axis=-1, keepdims=True)
    )
    scores = jnp.exp(scores - peak)
    fresh = jnp.exp(fresh - peak)
    denom = jnp.sum(scores, axis=-1, keepdims=True) + jnp.sum(fresh, axis=-1, keepdims=True)
    mixed = jnp.dot(scores.astype(jnp.bfloat16), v_ref[...], preferred_element_type=jnp.float32)
    mixed = mixed + jnp.dot(fresh.astype(jnp.bfloat16), fresh_v, preferred_element_type=jnp.float32)
    mixed = mixed / denom
    wide = jnp.concatenate([mixed[g * ROWS : (g + 1) * ROWS] for g in range(GROUP)], axis=1)
    attended[:, pl.ds(pl.multiple_of(head * GROUP * HD, GROUP * HD), GROUP * HD)] = wide


def attention_specs(denoise):
    return [
        smem_spec(),
        smem_spec(),
        pl.BlockSpec((None, None, ROWS, GROUP * HD), lambda h: (denoise, 0, 0, h)),
        pl.BlockSpec((None, CACHE, HD), lambda h: (0, 0, h)),
        pl.BlockSpec((None, CACHE, HD), lambda h: (0, 0, h)),
        pl.BlockSpec((2, None, ROWS, HD), lambda h: (0, 0, 0, h)),
        pl.BlockSpec((2, None, ROWS, HD), lambda h: (0, 0, 0, h)),
    ]


def first_attention(lengths, drift_rows, queries, keys, values, new_keys, new_values, block_in, drift_in, gain, ids):
    def body(lengths_ref, drift_ref, q_ref, k_ref, v_ref, nk_ref, nv_ref, block_ref, drift_in_ref, gain_ref, ids_ref,
             residual_ref, send_ref, bias, attended, spread, packed, counts):
        attend_head(0, lengths_ref, drift_ref, q_ref, k_ref, v_ref, nk_ref, nv_ref, bias, attended)

        @pl.when(pl.program_id(0) == KVH - 1)
        def _():
            inputs = jnp.concatenate(
                [block_ref[...].astype(jnp.float32), drift_in_ref[...].astype(jnp.float32)], axis=0
            )
            residual = inputs + attended[...]
            residual_ref[...] = residual
            dispatch(normalize(residual, gain_ref[...]), ids_ref, 0, counts, spread, packed, send_ref)

    return pl.pallas_call(
        body,
        grid=(KVH,),
        in_specs=attention_specs(0)
        + [
            pl.BlockSpec((None, BLOCK, D), lambda h: (0, 0, 0)),
            pl.BlockSpec((None, None, BLOCK, D), lambda h: (0, 0, 0, 0)),
            pl.BlockSpec((1, D), lambda h: (0, 0)),
            smem_spec(),
        ],
        out_specs=[
            pl.BlockSpec((ROWS, D), lambda h: (0, 0)),
            pl.BlockSpec((SLOTS, H, HD), lambda h: (0, 0, 0)),
        ],
        out_shape=[
            jax.ShapeDtypeStruct((ROWS, D), jnp.float32),
            jax.ShapeDtypeStruct((SLOTS, H, HD), jnp.bfloat16),
        ],
        scratch_shapes=[
            pltpu.VMEM((1, CACHE), jnp.float32),
            pltpu.VMEM((ROWS, D), jnp.float32),
            pltpu.VMEM((ROWS * H, HD), jnp.float32),
            pltpu.VMEM((ROWS, H, HD), jnp.bfloat16),
            pltpu.SMEM((EXPERTS,), jnp.int32),
        ],
        compiler_params=pltpu.CompilerParams(vmem_limit_bytes=56 * 1024 * 1024),
        name="first_attention",
    )(lengths, drift_rows, queries, keys, values, new_keys, new_values, block_in, drift_in, gain, ids)


def second_attention(lengths, drift_rows, queries, keys, values, new_keys, new_values):
    def body(lengths_ref, drift_ref, q_ref, k_ref, v_ref, nk_ref, nv_ref, attended, bias):
        attend_head(1, lengths_ref, drift_ref, q_ref, k_ref, v_ref, nk_ref, nv_ref, bias, attended)

    return pl.pallas_call(
        body,
        grid=(KVH,),
        in_specs=attention_specs(1),
        out_specs=pl.BlockSpec((ROWS, D), lambda h: (0, 0)),
        out_shape=jax.ShapeDtypeStruct((ROWS, D), jnp.float32),
        scratch_shapes=[pltpu.VMEM((1, CACHE), jnp.float32)],
        compiler_params=pltpu.CompilerParams(vmem_limit_bytes=VMEM_LIMIT),
        name="second_attention",
    )(lengths, drift_rows, queries, keys, values, new_keys, new_values)


def keep_in_vmem(weights):
    downs = weights[2:]
    shapes = (weights[0].shape, weights[1].shape, (sum(part.shape[0] for part in downs), D))

    def body(*refs):
        sources, (gate, up, down), sems = refs[: len(weights)], refs[len(weights) : -1], refs[-1]
        targets, row = [gate, up], 0
        for part in downs:
            targets.append(down.at[row : row + part.shape[0]])
            row += part.shape[0]
        copies = [
            pltpu.make_async_copy(source, target, sems.at[i])
            for i, (source, target) in enumerate(zip(sources, targets))
        ]
        for copy in copies:
            copy.start()
        for copy in copies:
            copy.wait()

    return pl.pallas_call(
        body,
        in_specs=[pl.BlockSpec(memory_space=pl.ANY)] * len(weights),
        out_specs=[pl.BlockSpec(memory_space=pltpu.VMEM)] * 3,
        out_shape=[pltpu.VMEM(shape, jnp.bfloat16) for shape in shapes],
        scratch_shapes=[pltpu.SemaphoreType.DMA((len(weights),))],
        compiler_params=pltpu.CompilerParams(vmem_limit_bytes=VMEM_LIMIT),
        name="keep_in_vmem",
    )(*weights)


def expert_half(rows, weights):
    pieces, count = len(weights), rows.shape[0]

    def body(*refs):
        rows_ref, weight_refs = refs[0], refs[1 : 1 + 3 * pieces]
        out_ref, flat, hidden = refs[1 + 3 * pieces :]
        for r in range(0, count, 16):
            wide = rows_ref[r : r + 16].astype(jnp.float32).reshape(16, D)
            flat[r : r + 16, :] = wide.astype(jnp.bfloat16)
        for p in range(pieces):
            gated = jnp.dot(flat[...], weight_refs[3 * p][...], preferred_element_type=jnp.float32)
            raised = jnp.dot(flat[...], weight_refs[3 * p + 1][...], preferred_element_type=jnp.float32)
            hidden[p] = (jax.nn.silu(gated) * raised).astype(jnp.bfloat16)
        width = 512
        heads = width // HD
        for n in range(D // width):
            part = jnp.zeros((count, width), jnp.float32)
            for p in range(pieces):
                part = part + jnp.dot(
                    hidden[p],
                    weight_refs[3 * p + 2][:, n * width : (n + 1) * width],
                    preferred_element_type=jnp.float32,
                )
            out_ref[:, n * heads : (n + 1) * heads, :] = part.reshape(count, heads, HD).astype(jnp.bfloat16)

    vmem = pl.BlockSpec(memory_space=pltpu.VMEM)
    return pl.pallas_call(
        body,
        in_specs=[vmem] * (1 + 3 * pieces),
        out_specs=vmem,
        out_shape=jax.ShapeDtypeStruct((count, H, HD), jnp.bfloat16),
        scratch_shapes=[
            pltpu.VMEM((count, D), jnp.bfloat16),
            pltpu.VMEM((pieces, count, QUARTER), jnp.bfloat16),
        ],
        compiler_params=pltpu.CompilerParams(vmem_limit_bytes=VMEM_LIMIT),
        name="expert_half",
    )(rows, *[part for piece in weights for part in piece])


def add_part(terms, away, part):
    steps = 2
    size = away.shape[0] // steps
    block = (size, H, HD)

    def body(terms_ref, away_ref, out_ref):
        total = terms_ref[...].astype(jnp.float32) + away_ref[...].astype(jnp.float32)
        out_ref[...] = total.astype(jnp.bfloat16)

    return pl.pallas_call(
        body,
        grid=(steps,),
        in_specs=[
            pl.BlockSpec(block, lambda i: (part * steps + i, 0, 0)),
            pl.BlockSpec(block, lambda i: (i, 0, 0)),
        ],
        out_specs=pl.BlockSpec(block, lambda i: (part * steps + i, 0, 0)),
        out_shape=jax.ShapeDtypeStruct(terms.shape, terms.dtype),
        input_output_aliases={0: 0},
        compiler_params=pltpu.CompilerParams(vmem_limit_bytes=VMEM_LIMIT),
        name="add_part",
    )(terms, away)


def combine_and_dispatch(terms, residual, attended, drift_in, gain, ids, gates):
    def body(terms_ref, residual_ref, attended_ref, drift_in_ref, gain_ref, ids_ref, gates_ref,
             result_ref, next_ref, send_ref, spread, packed, counts):
        moe = combine(terms_ref, ids_ref, gates_ref, 0, counts, spread)
        result = (residual_ref[...] + moe).astype(jnp.bfloat16)
        result_ref[...] = result
        inputs = jnp.concatenate(
            [result.astype(jnp.float32)[:BLOCK], drift_in_ref[1, 0].astype(jnp.float32)], axis=0
        )
        following = inputs + attended_ref[...]
        next_ref[...] = following
        dispatch(normalize(following, gain_ref[...]), ids_ref, 1, counts, spread, packed, send_ref)

    vmem = pl.BlockSpec(memory_space=pltpu.VMEM)
    return pl.pallas_call(
        body,
        in_specs=[vmem] * 5 + [smem_spec()] * 2,
        out_specs=[vmem] * 3,
        out_shape=[
            jax.ShapeDtypeStruct((ROWS, D), jnp.bfloat16),
            jax.ShapeDtypeStruct((ROWS, D), jnp.float32),
            jax.ShapeDtypeStruct((SLOTS, H, HD), jnp.bfloat16),
        ],
        scratch_shapes=[
            pltpu.VMEM((ROWS * H, HD), jnp.float32),
            pltpu.VMEM((ROWS, H, HD), jnp.bfloat16),
            pltpu.SMEM((EXPERTS,), jnp.int32),
        ],
        compiler_params=pltpu.CompilerParams(vmem_limit_bytes=VMEM_LIMIT),
        name="combine_and_dispatch",
    )(terms, residual, attended, drift_in, gain, ids, gates)


def combine_last(terms, residual, first_result, ids, gates):
    def body(terms_ref, residual_ref, first_ref, ids_ref, gates_ref, out_ref, spread, counts):
        moe = combine(terms_ref, ids_ref, gates_ref, 1, counts, spread)
        out_ref[0, 0] = first_ref[...]
        out_ref[1, 0] = (residual_ref[...] + moe).astype(jnp.bfloat16)

    vmem = pl.BlockSpec(memory_space=pltpu.VMEM)
    return pl.pallas_call(
        body,
        in_specs=[vmem] * 3 + [smem_spec()] * 2,
        out_specs=vmem,
        out_shape=jax.ShapeDtypeStruct((2, 1, ROWS, D), jnp.bfloat16),
        scratch_shapes=[
            pltpu.VMEM((ROWS * H, HD), jnp.float32),
            pltpu.SMEM((EXPERTS,), jnp.int32),
        ],
        compiler_params=pltpu.CompilerParams(vmem_limit_bytes=VMEM_LIMIT),
        name="combine_last",
    )(terms, residual, first_result, ids, gates)


def pairings(reps, exps):
    across, beside = [], []
    for r in range(reps):
        for e in range(exps):
            near, far = r ^ 1, reps - 1 - r
            if e % 2:
                near, far = far, near
            beside.append((r * exps + e, near * exps + e))
            across.append((r * exps + e, far * exps + e))
    return beside, across


def on_device(
    cache_keys,
    cache_values,
    lengths,
    drift_rows,
    block_in,
    drift_in,
    queries,
    new_keys,
    new_values,
    norm_gain,
    expert_ids,
    gate_weights,
    w_gate,
    w_up,
    w_down,
):
    axes = ("rep", "exp")
    beside, across = pairings(lax.axis_size("rep"), lax.axis_size("exp"))
    own = (w_gate[0], w_up[0], w_down[0])
    paired_gate, paired_up = (lax.ppermute(part, axes, beside) for part in own[:2])
    quarter = QUARTER // 4
    paired_gate, piece = lax.optimization_barrier((paired_gate, own[2][:quarter]))
    first_down = lax.ppermute(piece, axes, beside)
    paired_up, piece = lax.optimization_barrier((paired_up, own[2][quarter : 2 * quarter]))
    second_down = lax.ppermute(piece, axes, beside)
    first_down, piece = lax.optimization_barrier((first_down, own[2][2 * quarter :]))
    last_down = lax.ppermute(piece, axes, beside)
    paired = (paired_gate, paired_up, first_down, second_down, last_down)
    gain = norm_gain.reshape(1, D)
    expert_ids = jnp.swapaxes(expert_ids, 2, 3)
    gates = jnp.swapaxes(gate_weights, 2, 3).astype(jnp.float32)

    residual, send = first_attention(
        lengths, drift_rows, queries, cache_keys, cache_values, new_keys, new_values,
        block_in, drift_in, gain, expert_ids,
    )
    attended = second_attention(
        lengths, drift_rows, queries, cache_keys, cache_values, new_keys, new_values
    )

    weights = (keep_in_vmem(own), keep_in_vmem(paired))

    def experts(send, first):
        rows = lax.all_to_all(send, "exp", split_axis=0, concat_axis=0, tiled=True)
        rows, first = lax.optimization_barrier((rows, first))
        size = SLOTS // VISITS
        visiting = [lax.ppermute(rows[i * size : (i + 1) * size], axes, across) for i in range(VISITS)]
        away_terms = [lax.ppermute(expert_half(part, weights), axes, across) for part in visiting]
        terms = expert_half(rows, weights)
        for i, away in enumerate(away_terms):
            terms = add_part(terms, away, i)
        return lax.all_to_all(terms, "exp", split_axis=0, concat_axis=0, tiled=True), first

    terms, (_, attended, gates) = experts(send, (paired[:4], attended, gates))
    result, residual, send = combine_and_dispatch(
        terms, residual, attended, drift_in, gain, expert_ids, gates
    )
    terms, _ = experts(send, ())
    return combine_last(terms, residual, result, expert_ids, gates)


def solution(mesh):
    placed = (
        P(("rep", "exp"), None, None),
        P(("rep", "exp"), None, None),
        P(("rep", "exp")),
        P(None, ("rep", "exp"), None),
        P(("rep", "exp"), None, None),
        P(None, ("rep", "exp"), None, None),
        P(None, ("rep", "exp"), None, None),
        P(None, ("rep", "exp"), None, None),
        P(None, ("rep", "exp"), None, None),
        P(),
        P(None, ("rep", "exp"), None, None),
        P(None, ("rep", "exp"), None, None),
        P("exp", None, "rep"),
        P("exp", None, "rep"),
        P("exp", "rep", None),
    )
    return jax.shard_map(
        on_device,
        mesh=mesh,
        in_specs=placed,
        out_specs=P(None, ("rep", "exp"), None, None),
        check_vma=False,
    )
```

```python
import jax
import jax.numpy as jnp
from jax import lax
from jax.experimental import pallas as pl
from jax.experimental.pallas import tpu as pltpu
from jax.sharding import PartitionSpec as P

H = 32
KVH = 4
GROUP = H // KVH
HD = 128
D = H * HD
TOP = 8
BLOCK = 8
ROWS = 16
CAP = 3
EXPERTS = 64
SLOTS = EXPERTS * CAP
CACHE = 2048
QUARTER = 256
VISITS = 2
NEG = -1e30
VMEM_LIMIT = 24 * 1024 * 1024


def smem_spec():
    return pl.BlockSpec(memory_space=pltpu.SMEM)


def each_slot(ids_ref, denoise, counts, visit):
    for e in range(EXPERTS):
        counts[e] = 0

    @pl.loop(0, ROWS)
    def _(t):
        picked = []
        for j in range(TOP):
            e = ids_ref[denoise, 0, j, t]
            c = counts[e]
            counts[e] = c + 1
            picked.append(e * CAP + jnp.minimum(c, CAP - 1))
        visit(t, picked)


def slot_places(ids):
    def body(ids_ref, places_ref, counts):
        for denoise in range(2):

            def visit(t, picked):
                for j, slot in enumerate(picked):
                    places_ref[denoise, 0, j, t] = slot

            each_slot(ids_ref, denoise, counts, visit)

    return pl.pallas_call(
        body,
        in_specs=[smem_spec()],
        out_specs=smem_spec(),
        out_shape=jax.ShapeDtypeStruct(ids.shape, jnp.int32),
        scratch_shapes=[pltpu.SMEM((EXPERTS,), jnp.int32)],
        name="slot_places",
    )(ids)


def each_place(places_ref, denoise, visit):
    @pl.loop(0, ROWS, unroll=4)
    def _(t):
        visit(t, [places_ref[denoise, 0, j, t] for j in range(TOP)])


def normalize(residual, gain):
    inverse = lax.rsqrt(jnp.mean(residual * residual, axis=-1, keepdims=True) + 1e-06)
    return residual * inverse * gain


def dispatch(normed, walk, spread, packed, send_ref):
    for k in range(H):
        spread[pl.ds(k, ROWS, stride=H), :] = normed[:, k * HD : (k + 1) * HD]
    packed[...] = spread[...].reshape(ROWS, H, HD).astype(jnp.bfloat16)
    send_ref[...] = jnp.zeros_like(send_ref)

    def visit(t, picked):
        row = packed[t]
        for slot in picked:
            send_ref[slot] = row

    walk(visit)


def combine(terms_ref, places_ref, gates_ref, denoise, spread):
    def visit(t, picked):
        total = jnp.zeros((H, HD), jnp.float32)
        for j, slot in enumerate(picked):
            total = total + gates_ref[denoise, 0, j, t] * terms_ref[slot].astype(jnp.float32)
        spread[pl.ds(pl.multiple_of(t * H, H), H), :] = total

    each_place(places_ref, denoise, visit)
    return jnp.concatenate([spread[pl.ds(k, ROWS, stride=H), :] for k in range(H)], axis=1)


def attend_head(denoise, lengths_ref, drift_ref, q_ref, k_ref, v_ref, nk_ref, nv_ref, bias, attended):
    head = pl.program_id(0)
    extra = ROWS * (denoise + 1)

    @pl.when(head == 0)
    def _():
        place = lax.broadcasted_iota(jnp.int32, (1, CACHE), 1)
        admitted = place < lengths_ref[0]
        for step in range(denoise + 1):
            for b in range(BLOCK):
                admitted = admitted & (place != drift_ref[step, 0, b])
        bias[...] = jnp.where(admitted, 0.0, NEG)

    queries = jnp.concatenate([q_ref[:, g * HD : (g + 1) * HD] for g in range(GROUP)], axis=0)
    contract_last = (((1,), (1,)), ((), ()))
    scale = HD ** (-0.5)
    scores = lax.dot_general(queries, k_ref[...], contract_last, preferred_element_type=jnp.float32)
    scores = scores * scale + bias[...]
    fresh_k = nk_ref[0 : denoise + 1].reshape(extra, HD)
    fresh_v = nv_ref[0 : denoise + 1].reshape(extra, HD)
    fresh = lax.dot_general(queries, fresh_k, contract_last, preferred_element_type=jnp.float32)
    row = lax.broadcasted_iota(jnp.int32, (GROUP * ROWS, extra), 0)
    col = lax.broadcasted_iota(jnp.int32, (GROUP * ROWS, extra), 1)
    place = col % ROWS
    allowed = (col >= denoise * ROWS) & ((place >= BLOCK) | (row % ROWS < BLOCK))
    if denoise == 1:
        for b in range(BLOCK):
            kept = drift_ref[1, 0, 0] != drift_ref[0, 0, b]
            for other in range(1, BLOCK):
                kept = kept & (drift_ref[1, 0, other] != drift_ref[0, 0, b])
            allowed = allowed | ((col == BLOCK + b) & kept)
    fresh = jnp.where(allowed, fresh * scale, NEG)
    peak = jnp.maximum(
        jnp.max(scores, axis=-1, keepdims=True), jnp.max(fresh, axis=-1, keepdims=True)
    )
    scores = jnp.exp(scores - peak)
    fresh = jnp.exp(fresh - peak)
    denom = jnp.sum(scores, axis=-1, keepdims=True) + jnp.sum(fresh, axis=-1, keepdims=True)
    mixed = jnp.dot(scores.astype(jnp.bfloat16), v_ref[...], preferred_element_type=jnp.float32)
    mixed = mixed + jnp.dot(fresh.astype(jnp.bfloat16), fresh_v, preferred_element_type=jnp.float32)
    mixed = mixed / denom
    wide = jnp.concatenate([mixed[g * ROWS : (g + 1) * ROWS] for g in range(GROUP)], axis=1)
    attended[:, pl.ds(pl.multiple_of(head * GROUP * HD, GROUP * HD), GROUP * HD)] = wide


def attention_specs(denoise):
    return [
        smem_spec(),
        smem_spec(),
        pl.BlockSpec((None, None, ROWS, GROUP * HD), lambda h: (denoise, 0, 0, h)),
        pl.BlockSpec((None, CACHE, HD), lambda h: (0, 0, h)),
        pl.BlockSpec((None, CACHE, HD), lambda h: (0, 0, h)),
        pl.BlockSpec((2, None, ROWS, HD), lambda h: (0, 0, 0, h)),
        pl.BlockSpec((2, None, ROWS, HD), lambda h: (0, 0, 0, h)),
    ]


def first_attention(lengths, drift_rows, queries, keys, values, new_keys, new_values, block_in, drift_in, gain, ids):
    def body(lengths_ref, drift_ref, q_ref, k_ref, v_ref, nk_ref, nv_ref, block_ref, drift_in_ref, gain_ref, ids_ref,
             residual_ref, send_ref, bias, attended, spread, packed, counts):
        attend_head(0, lengths_ref, drift_ref, q_ref, k_ref, v_ref, nk_ref, nv_ref, bias, attended)

        @pl.when(pl.program_id(0) == KVH - 1)
        def _():
            inputs = jnp.concatenate(
                [block_ref[...].astype(jnp.float32), drift_in_ref[...].astype(jnp.float32)], axis=0
            )
            residual = inputs + attended[...]
            residual_ref[...] = residual
            walk = lambda visit: each_slot(ids_ref, 0, counts, visit)
            dispatch(normalize(residual, gain_ref[...]), walk, spread, packed, send_ref)

    return pl.pallas_call(
        body,
        grid=(KVH,),
        in_specs=attention_specs(0)
        + [
            pl.BlockSpec((None, BLOCK, D), lambda h: (0, 0, 0)),
            pl.BlockSpec((None, None, BLOCK, D), lambda h: (0, 0, 0, 0)),
            pl.BlockSpec((1, D), lambda h: (0, 0)),
            smem_spec(),
        ],
        out_specs=[
            pl.BlockSpec((ROWS, D), lambda h: (0, 0)),
            pl.BlockSpec((SLOTS, H, HD), lambda h: (0, 0, 0)),
        ],
        out_shape=[
            jax.ShapeDtypeStruct((ROWS, D), jnp.float32),
            jax.ShapeDtypeStruct((SLOTS, H, HD), jnp.bfloat16),
        ],
        scratch_shapes=[
            pltpu.VMEM((1, CACHE), jnp.float32),
            pltpu.VMEM((ROWS, D), jnp.float32),
            pltpu.VMEM((ROWS * H, HD), jnp.float32),
            pltpu.VMEM((ROWS, H, HD), jnp.bfloat16),
            pltpu.SMEM((EXPERTS,), jnp.int32),
        ],
        compiler_params=pltpu.CompilerParams(vmem_limit_bytes=56 * 1024 * 1024),
        name="first_attention",
    )(lengths, drift_rows, queries, keys, values, new_keys, new_values, block_in, drift_in, gain, ids)


def second_attention(lengths, drift_rows, queries, keys, values, new_keys, new_values):
    def body(lengths_ref, drift_ref, q_ref, k_ref, v_ref, nk_ref, nv_ref, attended, bias):
        attend_head(1, lengths_ref, drift_ref, q_ref, k_ref, v_ref, nk_ref, nv_ref, bias, attended)

    return pl.pallas_call(
        body,
        grid=(KVH,),
        in_specs=attention_specs(1),
        out_specs=pl.BlockSpec((ROWS, D), lambda h: (0, 0)),
        out_shape=jax.ShapeDtypeStruct((ROWS, D), jnp.float32),
        scratch_shapes=[pltpu.VMEM((1, CACHE), jnp.float32)],
        compiler_params=pltpu.CompilerParams(vmem_limit_bytes=VMEM_LIMIT),
        name="second_attention",
    )(lengths, drift_rows, queries, keys, values, new_keys, new_values)


def keep_in_vmem(weights):
    downs = weights[2:]
    shapes = (weights[0].shape, weights[1].shape, (sum(part.shape[0] for part in downs), D))

    def body(*refs):
        sources, (gate, up, down), sems = refs[: len(weights)], refs[len(weights) : -1], refs[-1]
        targets, row = [gate, up], 0
        for part in downs:
            targets.append(down.at[row : row + part.shape[0]])
            row += part.shape[0]
        copies = [
            pltpu.make_async_copy(source, target, sems.at[i])
            for i, (source, target) in enumerate(zip(sources, targets))
        ]
        for copy in copies:
            copy.start()
        for copy in copies:
            copy.wait()

    return pl.pallas_call(
        body,
        in_specs=[pl.BlockSpec(memory_space=pl.ANY)] * len(weights),
        out_specs=[pl.BlockSpec(memory_space=pltpu.VMEM)] * 3,
        out_shape=[pltpu.VMEM(shape, jnp.bfloat16) for shape in shapes],
        scratch_shapes=[pltpu.SemaphoreType.DMA((len(weights),))],
        compiler_params=pltpu.CompilerParams(vmem_limit_bytes=VMEM_LIMIT),
        name="keep_in_vmem",
    )(*weights)


def expert_half(rows, weights):
    pieces, count = len(weights), rows.shape[0]

    def body(*refs):
        rows_ref, weight_refs = refs[0], refs[1 : 1 + 3 * pieces]
        out_ref, flat, hidden = refs[1 + 3 * pieces :]
        for r in range(0, count, 16):
            wide = rows_ref[r : r + 16].astype(jnp.float32).reshape(16, D)
            flat[r : r + 16, :] = wide.astype(jnp.bfloat16)
        for p in range(pieces):
            gated = jnp.dot(flat[...], weight_refs[3 * p][...], preferred_element_type=jnp.float32)
            raised = jnp.dot(flat[...], weight_refs[3 * p + 1][...], preferred_element_type=jnp.float32)
            hidden[p] = (jax.nn.silu(gated) * raised).astype(jnp.bfloat16)
        width = 512
        heads = width // HD
        for n in range(D // width):
            part = jnp.zeros((count, width), jnp.float32)
            for p in range(pieces):
                part = part + jnp.dot(
                    hidden[p],
                    weight_refs[3 * p + 2][:, n * width : (n + 1) * width],
                    preferred_element_type=jnp.float32,
                )
            out_ref[:, n * heads : (n + 1) * heads, :] = part.reshape(count, heads, HD).astype(jnp.bfloat16)

    vmem = pl.BlockSpec(memory_space=pltpu.VMEM)
    return pl.pallas_call(
        body,
        in_specs=[vmem] * (1 + 3 * pieces),
        out_specs=vmem,
        out_shape=jax.ShapeDtypeStruct((count, H, HD), jnp.bfloat16),
        scratch_shapes=[
            pltpu.VMEM((count, D), jnp.bfloat16),
            pltpu.VMEM((pieces, count, QUARTER), jnp.bfloat16),
        ],
        compiler_params=pltpu.CompilerParams(vmem_limit_bytes=VMEM_LIMIT),
        name="expert_half",
    )(rows, *[part for piece in weights for part in piece])


def add_part(terms, away, part):
    steps = 2
    size = away.shape[0] // steps
    block = (size, H, HD)

    def body(terms_ref, away_ref, out_ref):
        total = terms_ref[...].astype(jnp.float32) + away_ref[...].astype(jnp.float32)
        out_ref[...] = total.astype(jnp.bfloat16)

    return pl.pallas_call(
        body,
        grid=(steps,),
        in_specs=[
            pl.BlockSpec(block, lambda i: (part * steps + i, 0, 0)),
            pl.BlockSpec(block, lambda i: (i, 0, 0)),
        ],
        out_specs=pl.BlockSpec(block, lambda i: (part * steps + i, 0, 0)),
        out_shape=jax.ShapeDtypeStruct(terms.shape, terms.dtype),
        input_output_aliases={0: 0},
        compiler_params=pltpu.CompilerParams(vmem_limit_bytes=VMEM_LIMIT),
        name="add_part",
    )(terms, away)


def combine_and_dispatch(terms, residual, attended, drift_in, gain, places, gates):
    def body(terms_ref, residual_ref, attended_ref, drift_in_ref, gain_ref, places_ref, gates_ref,
             out_ref, next_ref, send_ref, spread, packed):
        moe = combine(terms_ref, places_ref, gates_ref, 0, spread)
        result = (residual_ref[...] + moe).astype(jnp.bfloat16)
        out_ref[0, 0] = result
        inputs = jnp.concatenate(
            [result.astype(jnp.float32)[:BLOCK], drift_in_ref[1, 0].astype(jnp.float32)], axis=0
        )
        following = inputs + attended_ref[...]
        next_ref[...] = following
        walk = lambda visit: each_place(places_ref, 1, visit)
        dispatch(normalize(following, gain_ref[...]), walk, spread, packed, send_ref)

    vmem = pl.BlockSpec(memory_space=pltpu.VMEM)
    first_half = pl.BlockSpec((1, 1, ROWS, D), lambda i: (0, 0, 0, 0))
    return pl.pallas_call(
        body,
        grid=(1,),
        in_specs=[vmem] * 5 + [smem_spec()] * 2,
        out_specs=[first_half, vmem, vmem],
        out_shape=[
            jax.ShapeDtypeStruct((2, 1, ROWS, D), jnp.bfloat16),
            jax.ShapeDtypeStruct((ROWS, D), jnp.float32),
            jax.ShapeDtypeStruct((SLOTS, H, HD), jnp.bfloat16),
        ],
        scratch_shapes=[
            pltpu.VMEM((ROWS * H, HD), jnp.float32),
            pltpu.VMEM((ROWS, H, HD), jnp.bfloat16),
        ],
        compiler_params=pltpu.CompilerParams(vmem_limit_bytes=VMEM_LIMIT),
        name="combine_and_dispatch",
    )(terms, residual, attended, drift_in, gain, places, gates)


def combine_last(terms, residual, output, places, gates):
    def body(terms_ref, residual_ref, output_ref, places_ref, gates_ref, out_ref, spread):
        moe = combine(terms_ref, places_ref, gates_ref, 1, spread)
        out_ref[0, 0] = (residual_ref[...] + moe).astype(jnp.bfloat16)

    vmem = pl.BlockSpec(memory_space=pltpu.VMEM)
    return pl.pallas_call(
        body,
        grid=(1,),
        in_specs=[vmem] * 2 + [pl.BlockSpec(memory_space=pl.ANY)] + [smem_spec()] * 2,
        out_specs=pl.BlockSpec((1, 1, ROWS, D), lambda i: (1, 0, 0, 0)),
        out_shape=jax.ShapeDtypeStruct(output.shape, output.dtype),
        input_output_aliases={2: 0},
        scratch_shapes=[pltpu.VMEM((ROWS * H, HD), jnp.float32)],
        compiler_params=pltpu.CompilerParams(vmem_limit_bytes=VMEM_LIMIT),
        name="combine_last",
    )(terms, residual, output, places, gates)


def pairings(reps, exps):
    across, beside = [], []
    for r in range(reps):
        for e in range(exps):
            near, far = r ^ 1, reps - 1 - r
            if e % 2:
                near, far = far, near
            beside.append((r * exps + e, near * exps + e))
            across.append((r * exps + e, far * exps + e))
    return beside, across


def on_device(
    cache_keys,
    cache_values,
    lengths,
    drift_rows,
    block_in,
    drift_in,
    queries,
    new_keys,
    new_values,
    norm_gain,
    expert_ids,
    gate_weights,
    w_gate,
    w_up,
    w_down,
):
    axes = ("rep", "exp")
    beside, across = pairings(lax.axis_size("rep"), lax.axis_size("exp"))
    own = (w_gate[0], w_up[0], w_down[0])
    gate_up = [lax.ppermute(part, axes, beside) for part in own[:2]]
    downs = []
    for i, half in enumerate(jnp.split(own[2], 2)):
        gate_up[i], half = lax.optimization_barrier((gate_up[i], half))
        downs.append(lax.ppermute(half, axes, beside))
    paired = (*gate_up, *downs)
    gain = norm_gain.reshape(1, D)
    expert_ids = jnp.swapaxes(expert_ids, 2, 3)
    gates = jnp.swapaxes(gate_weights, 2, 3).astype(jnp.float32)

    residual, send = first_attention(
        lengths, drift_rows, queries, cache_keys, cache_values, new_keys, new_values,
        block_in, drift_in, gain, expert_ids,
    )
    attended = second_attention(
        lengths, drift_rows, queries, cache_keys, cache_values, new_keys, new_values
    )

    weights = (keep_in_vmem(own), keep_in_vmem(paired))

    def experts(send, first):
        rows = lax.all_to_all(send, "exp", split_axis=0, concat_axis=0, tiled=True)
        rows, first = lax.optimization_barrier((rows, first))
        size = SLOTS // VISITS
        visiting = [lax.ppermute(rows[i * size : (i + 1) * size], axes, across) for i in range(VISITS)]
        away_terms = [lax.ppermute(expert_half(part, weights), axes, across) for part in visiting]
        terms = expert_half(rows, weights)
        for i, away in enumerate(away_terms):
            terms = add_part(terms, away, i)
        return lax.all_to_all(terms, "exp", split_axis=0, concat_axis=0, tiled=True), first

    terms, (_, attended, gates, places) = experts(
        send, (paired, attended, gates, slot_places(expert_ids))
    )
    output, residual, send = combine_and_dispatch(
        terms, residual, attended, drift_in, gain, places, gates
    )
    terms, _ = experts(send, ())
    return combine_last(terms, residual, output, places, gates)


def solution(mesh):
    placed = (
        P(("rep", "exp"), None, None),
        P(("rep", "exp"), None, None),
        P(("rep", "exp")),
        P(None, ("rep", "exp"), None),
        P(("rep", "exp"), None, None),
        P(None, ("rep", "exp"), None, None),
        P(None, ("rep", "exp"), None, None),
        P(None, ("rep", "exp"), None, None),
        P(None, ("rep", "exp"), None, None),
        P(),
        P(None, ("rep", "exp"), None, None),
        P(None, ("rep", "exp"), None, None),
        P("exp", None, "rep"),
        P("exp", None, "rep"),
        P("exp", "rep", None),
    )
    return jax.shard_map(
        on_device,
        mesh=mesh,
        in_specs=placed,
        out_specs=P(None, ("rep", "exp"), None, None),
        check_vma=False,
    )
```

```python
import jax
import jax.numpy as jnp
from jax import lax
from jax.experimental import pallas as pl
from jax.experimental.pallas import tpu as pltpu
from jax.sharding import PartitionSpec as P

H = 32
KVH = 4
GROUP = H // KVH
HD = 128
D = H * HD
TOP = 8
BLOCK = 8
ROWS = 16
CAP = 3
EXPERTS = 64
SLOTS = EXPERTS * CAP
CACHE = 2048
QUARTER = 256
VISITS = 2
NEG = -1e30
VMEM_LIMIT = 24 * 1024 * 1024


def smem_spec():
    return pl.BlockSpec(memory_space=pltpu.SMEM)


def each_slot(ids_ref, denoise, counts, visit):
    for e in range(EXPERTS):
        counts[e] = 0

    @pl.loop(0, ROWS)
    def _(t):
        picked = []
        for j in range(TOP):
            e = ids_ref[denoise, 0, j, t]
            c = counts[e]
            counts[e] = c + 1
            picked.append(e * CAP + jnp.minimum(c, CAP - 1))
        visit(t, picked)


def slot_places(ids):
    def body(ids_ref, places_ref, counts):
        for denoise in range(2):

            def visit(t, picked):
                for j, slot in enumerate(picked):
                    places_ref[denoise, 0, j, t] = slot

            each_slot(ids_ref, denoise, counts, visit)

    return pl.pallas_call(
        body,
        in_specs=[smem_spec()],
        out_specs=smem_spec(),
        out_shape=jax.ShapeDtypeStruct(ids.shape, jnp.int32),
        scratch_shapes=[pltpu.SMEM((EXPERTS,), jnp.int32)],
        name="slot_places",
    )(ids)


def each_place(places_ref, denoise, visit):
    for t in range(ROWS):
        visit(t, [places_ref[denoise, 0, j, t] for j in range(TOP)])


def normalize(residual, gain):
    inverse = lax.rsqrt(jnp.mean(residual * residual, axis=-1, keepdims=True) + 1e-06)
    return residual * inverse * gain


def dispatch(normed, walk, spread, packed, send_ref):
    for k in range(H):
        spread[pl.ds(k, ROWS, stride=H), :] = normed[:, k * HD : (k + 1) * HD]
    packed[...] = spread[...].reshape(ROWS, H, HD).astype(jnp.bfloat16)
    send_ref[...] = jnp.zeros_like(send_ref)

    def visit(t, picked):
        row = packed[t]
        for slot in picked:
            send_ref[slot] = row

    walk(visit)


def combine(terms_ref, places_ref, gates_ref, denoise, spread):
    def visit(t, picked):
        shares = [
            gates_ref[denoise, 0, j, t] * terms_ref[slot].astype(jnp.float32)
            for j, slot in enumerate(picked)
        ]
        while len(shares) > 1:
            shares = [a + b for a, b in zip(shares[::2], shares[1::2])]
        spread[t * H : (t + 1) * H, :] = shares[0]

    each_place(places_ref, denoise, visit)
    return jnp.concatenate([spread[pl.ds(k, ROWS, stride=H), :] for k in range(H)], axis=1)


def attend_head(denoise, lengths_ref, drift_ref, q_ref, k_ref, v_ref, nk_ref, nv_ref, bias, attended):
    head = pl.program_id(0)
    extra = ROWS * (denoise + 1)

    @pl.when(head == 0)
    def _():
        place = lax.broadcasted_iota(jnp.int32, (1, CACHE), 1)
        admitted = place < lengths_ref[0]
        for step in range(denoise + 1):
            for b in range(BLOCK):
                admitted = admitted & (place != drift_ref[step, 0, b])
        bias[...] = jnp.where(admitted, 0.0, NEG)

    queries = jnp.concatenate([q_ref[:, g * HD : (g + 1) * HD] for g in range(GROUP)], axis=0)
    contract_last = (((1,), (1,)), ((), ()))
    scale = HD ** (-0.5)
    scores = lax.dot_general(queries, k_ref[...], contract_last, preferred_element_type=jnp.float32)
    scores = scores * scale + bias[...]
    fresh_k = nk_ref[0 : denoise + 1].reshape(extra, HD)
    fresh_v = nv_ref[0 : denoise + 1].reshape(extra, HD)
    fresh = lax.dot_general(queries, fresh_k, contract_last, preferred_element_type=jnp.float32)
    row = lax.broadcasted_iota(jnp.int32, (GROUP * ROWS, extra), 0)
    col = lax.broadcasted_iota(jnp.int32, (GROUP * ROWS, extra), 1)
    place = col % ROWS
    allowed = (col >= denoise * ROWS) & ((place >= BLOCK) | (row % ROWS < BLOCK))
    if denoise == 1:
        for b in range(BLOCK):
            kept = drift_ref[1, 0, 0] != drift_ref[0, 0, b]
            for other in range(1, BLOCK):
                kept = kept & (drift_ref[1, 0, other] != drift_ref[0, 0, b])
            allowed = allowed | ((col == BLOCK + b) & kept)
    fresh = jnp.where(allowed, fresh * scale, NEG)
    peak = jnp.maximum(
        jnp.max(scores, axis=-1, keepdims=True), jnp.max(fresh, axis=-1, keepdims=True)
    )
    scores = jnp.exp(scores - peak)
    fresh = jnp.exp(fresh - peak)
    denom = jnp.sum(scores, axis=-1, keepdims=True) + jnp.sum(fresh, axis=-1, keepdims=True)
    mixed = jnp.dot(scores.astype(jnp.bfloat16), v_ref[...], preferred_element_type=jnp.float32)
    mixed = mixed + jnp.dot(fresh.astype(jnp.bfloat16), fresh_v, preferred_element_type=jnp.float32)
    mixed = mixed / denom
    wide = jnp.concatenate([mixed[g * ROWS : (g + 1) * ROWS] for g in range(GROUP)], axis=1)
    attended[:, pl.ds(pl.multiple_of(head * GROUP * HD, GROUP * HD), GROUP * HD)] = wide


def attention_specs(denoise):
    return [
        smem_spec(),
        smem_spec(),
        pl.BlockSpec((None, None, ROWS, GROUP * HD), lambda h: (denoise, 0, 0, h)),
        pl.BlockSpec((None, CACHE, HD), lambda h: (0, 0, h)),
        pl.BlockSpec((None, CACHE, HD), lambda h: (0, 0, h)),
        pl.BlockSpec((2, None, ROWS, HD), lambda h: (0, 0, 0, h)),
        pl.BlockSpec((2, None, ROWS, HD), lambda h: (0, 0, 0, h)),
    ]


def first_attention(lengths, drift_rows, queries, keys, values, new_keys, new_values, block_in, drift_in, gain, ids):
    def body(lengths_ref, drift_ref, q_ref, k_ref, v_ref, nk_ref, nv_ref, block_ref, drift_in_ref, gain_ref, ids_ref,
             residual_ref, send_ref, bias, attended, spread, packed, counts):
        attend_head(0, lengths_ref, drift_ref, q_ref, k_ref, v_ref, nk_ref, nv_ref, bias, attended)

        @pl.when(pl.program_id(0) == KVH - 1)
        def _():
            inputs = jnp.concatenate(
                [block_ref[...].astype(jnp.float32), drift_in_ref[...].astype(jnp.float32)], axis=0
            )
            residual = inputs + attended[...]
            residual_ref[...] = residual
            walk = lambda visit: each_slot(ids_ref, 0, counts, visit)
            dispatch(normalize(residual, gain_ref[...]), walk, spread, packed, send_ref)

    return pl.pallas_call(
        body,
        grid=(KVH,),
        in_specs=attention_specs(0)
        + [
            pl.BlockSpec((None, BLOCK, D), lambda h: (0, 0, 0)),
            pl.BlockSpec((None, None, BLOCK, D), lambda h: (0, 0, 0, 0)),
            pl.BlockSpec((1, D), lambda h: (0, 0)),
            smem_spec(),
        ],
        out_specs=[
            pl.BlockSpec((ROWS, D), lambda h: (0, 0)),
            pl.BlockSpec((SLOTS, H, HD), lambda h: (0, 0, 0)),
        ],
        out_shape=[
            jax.ShapeDtypeStruct((ROWS, D), jnp.float32),
            jax.ShapeDtypeStruct((SLOTS, H, HD), jnp.bfloat16),
        ],
        scratch_shapes=[
            pltpu.VMEM((1, CACHE), jnp.float32),
            pltpu.VMEM((ROWS, D), jnp.float32),
            pltpu.VMEM((ROWS * H, HD), jnp.float32),
            pltpu.VMEM((ROWS, H, HD), jnp.bfloat16),
            pltpu.SMEM((EXPERTS,), jnp.int32),
        ],
        compiler_params=pltpu.CompilerParams(vmem_limit_bytes=56 * 1024 * 1024),
        name="first_attention",
    )(lengths, drift_rows, queries, keys, values, new_keys, new_values, block_in, drift_in, gain, ids)


def second_attention(lengths, drift_rows, queries, keys, values, new_keys, new_values):
    def body(lengths_ref, drift_ref, q_ref, k_ref, v_ref, nk_ref, nv_ref, attended, bias):
        attend_head(1, lengths_ref, drift_ref, q_ref, k_ref, v_ref, nk_ref, nv_ref, bias, attended)

    return pl.pallas_call(
        body,
        grid=(KVH,),
        in_specs=attention_specs(1),
        out_specs=pl.BlockSpec((ROWS, D), lambda h: (0, 0)),
        out_shape=jax.ShapeDtypeStruct((ROWS, D), jnp.float32),
        scratch_shapes=[pltpu.VMEM((1, CACHE), jnp.float32)],
        compiler_params=pltpu.CompilerParams(vmem_limit_bytes=VMEM_LIMIT),
        name="second_attention",
    )(lengths, drift_rows, queries, keys, values, new_keys, new_values)


def keep_in_vmem(weights):
    downs = weights[2:]
    shapes = (weights[0].shape, weights[1].shape, (sum(part.shape[0] for part in downs), D))

    def body(*refs):
        sources, (gate, up, down), sems = refs[: len(weights)], refs[len(weights) : -1], refs[-1]
        targets, row = [gate, up], 0
        for part in downs:
            targets.append(down.at[row : row + part.shape[0]])
            row += part.shape[0]
        copies = [
            pltpu.make_async_copy(source, target, sems.at[i])
            for i, (source, target) in enumerate(zip(sources, targets))
        ]
        for copy in copies:
            copy.start()
        for copy in copies:
            copy.wait()

    return pl.pallas_call(
        body,
        in_specs=[pl.BlockSpec(memory_space=pl.ANY)] * len(weights),
        out_specs=[pl.BlockSpec(memory_space=pltpu.VMEM)] * 3,
        out_shape=[pltpu.VMEM(shape, jnp.bfloat16) for shape in shapes],
        scratch_shapes=[pltpu.SemaphoreType.DMA((len(weights),))],
        compiler_params=pltpu.CompilerParams(vmem_limit_bytes=VMEM_LIMIT),
        name="keep_in_vmem",
    )(*weights)


def expert_half(rows, weights):
    pieces, count = len(weights), rows.shape[0]

    def body(*refs):
        rows_ref, weight_refs = refs[0], refs[1 : 1 + 3 * pieces]
        out_ref, flat, hidden = refs[1 + 3 * pieces :]
        for r in range(0, count, 16):
            wide = rows_ref[r : r + 16].astype(jnp.float32).reshape(16, D)
            flat[r : r + 16, :] = wide.astype(jnp.bfloat16)
        for p in range(pieces):
            gated = jnp.dot(flat[...], weight_refs[3 * p][...], preferred_element_type=jnp.float32)
            raised = jnp.dot(flat[...], weight_refs[3 * p + 1][...], preferred_element_type=jnp.float32)
            hidden[p] = (jax.nn.silu(gated) * raised).astype(jnp.bfloat16)
        width = 512
        heads = width // HD
        for n in range(D // width):
            part = jnp.zeros((count, width), jnp.float32)
            for p in range(pieces):
                part = part + jnp.dot(
                    hidden[p],
                    weight_refs[3 * p + 2][:, n * width : (n + 1) * width],
                    preferred_element_type=jnp.float32,
                )
            out_ref[:, n * heads : (n + 1) * heads, :] = part.reshape(count, heads, HD).astype(jnp.bfloat16)

    vmem = pl.BlockSpec(memory_space=pltpu.VMEM)
    return pl.pallas_call(
        body,
        in_specs=[vmem] * (1 + 3 * pieces),
        out_specs=vmem,
        out_shape=jax.ShapeDtypeStruct((count, H, HD), jnp.bfloat16),
        scratch_shapes=[
            pltpu.VMEM((count, D), jnp.bfloat16),
            pltpu.VMEM((pieces, count, QUARTER), jnp.bfloat16),
        ],
        compiler_params=pltpu.CompilerParams(vmem_limit_bytes=VMEM_LIMIT),
        name="expert_half",
    )(rows, *[part for piece in weights for part in piece])


def add_part(terms, away, part):
    steps = 2
    size = away.shape[0] // steps
    block = (size, H, HD)

    def body(terms_ref, away_ref, out_ref):
        total = terms_ref[...].astype(jnp.float32) + away_ref[...].astype(jnp.float32)
        out_ref[...] = total.astype(jnp.bfloat16)

    return pl.pallas_call(
        body,
        grid=(steps,),
        in_specs=[
            pl.BlockSpec(block, lambda i: (part * steps + i, 0, 0)),
            pl.BlockSpec(block, lambda i: (i, 0, 0)),
        ],
        out_specs=pl.BlockSpec(block, lambda i: (part * steps + i, 0, 0)),
        out_shape=jax.ShapeDtypeStruct(terms.shape, terms.dtype),
        input_output_aliases={0: 0},
        compiler_params=pltpu.CompilerParams(vmem_limit_bytes=VMEM_LIMIT),
        name="add_part",
    )(terms, away)


def combine_and_dispatch(terms, residual, attended, drift_in, gain, places, gates):
    def body(terms_ref, residual_ref, attended_ref, drift_in_ref, gain_ref, places_ref, gates_ref,
             out_ref, next_ref, send_ref, spread, packed):
        moe = combine(terms_ref, places_ref, gates_ref, 0, spread)
        result = (residual_ref[...] + moe).astype(jnp.bfloat16)
        out_ref[0, 0] = result
        inputs = jnp.concatenate(
            [result.astype(jnp.float32)[:BLOCK], drift_in_ref[1, 0].astype(jnp.float32)], axis=0
        )
        following = inputs + attended_ref[...]
        next_ref[...] = following
        walk = lambda visit: each_place(places_ref, 1, visit)
        dispatch(normalize(following, gain_ref[...]), walk, spread, packed, send_ref)

    vmem = pl.BlockSpec(memory_space=pltpu.VMEM)
    first_half = pl.BlockSpec((1, 1, ROWS, D), lambda i: (0, 0, 0, 0))
    return pl.pallas_call(
        body,
        grid=(1,),
        in_specs=[vmem] * 5 + [smem_spec()] * 2,
        out_specs=[first_half, vmem, vmem],
        out_shape=[
            jax.ShapeDtypeStruct((2, 1, ROWS, D), jnp.bfloat16),
            jax.ShapeDtypeStruct((ROWS, D), jnp.float32),
            jax.ShapeDtypeStruct((SLOTS, H, HD), jnp.bfloat16),
        ],
        scratch_shapes=[
            pltpu.VMEM((ROWS * H, HD), jnp.float32),
            pltpu.VMEM((ROWS, H, HD), jnp.bfloat16),
        ],
        compiler_params=pltpu.CompilerParams(vmem_limit_bytes=VMEM_LIMIT),
        name="combine_and_dispatch",
    )(terms, residual, attended, drift_in, gain, places, gates)


def combine_last(terms, residual, output, places, gates):
    def body(terms_ref, residual_ref, output_ref, places_ref, gates_ref, out_ref, spread):
        moe = combine(terms_ref, places_ref, gates_ref, 1, spread)
        out_ref[0, 0] = (residual_ref[...] + moe).astype(jnp.bfloat16)

    vmem = pl.BlockSpec(memory_space=pltpu.VMEM)
    return pl.pallas_call(
        body,
        grid=(1,),
        in_specs=[vmem] * 2 + [pl.BlockSpec(memory_space=pl.ANY)] + [smem_spec()] * 2,
        out_specs=pl.BlockSpec((1, 1, ROWS, D), lambda i: (1, 0, 0, 0)),
        out_shape=jax.ShapeDtypeStruct(output.shape, output.dtype),
        input_output_aliases={2: 0},
        scratch_shapes=[pltpu.VMEM((ROWS * H, HD), jnp.float32)],
        compiler_params=pltpu.CompilerParams(vmem_limit_bytes=VMEM_LIMIT),
        name="combine_last",
    )(terms, residual, output, places, gates)


def pairings(reps, exps):
    across, beside = [], []
    for r in range(reps):
        for e in range(exps):
            near, far = r ^ 1, reps - 1 - r
            if e % 2:
                near, far = far, near
            beside.append((r * exps + e, near * exps + e))
            across.append((r * exps + e, far * exps + e))
    return beside, across


def on_device(
    cache_keys,
    cache_values,
    lengths,
    drift_rows,
    block_in,
    drift_in,
    queries,
    new_keys,
    new_values,
    norm_gain,
    expert_ids,
    gate_weights,
    w_gate,
    w_up,
    w_down,
):
    axes = ("rep", "exp")
    beside, across = pairings(lax.axis_size("rep"), lax.axis_size("exp"))
    own = (w_gate[0], w_up[0], w_down[0])
    gate_up = [lax.ppermute(part, axes, beside) for part in own[:2]]
    downs = []
    for i, half in enumerate(jnp.split(own[2], 2)):
        gate_up[i], half = lax.optimization_barrier((gate_up[i], half))
        downs.append(lax.ppermute(half, axes, beside))
    paired = (*gate_up, *downs)
    gain = norm_gain.reshape(1, D)
    expert_ids = jnp.swapaxes(expert_ids, 2, 3)
    gates = jnp.swapaxes(gate_weights, 2, 3).astype(jnp.float32)

    residual, send = first_attention(
        lengths, drift_rows, queries, cache_keys, cache_values, new_keys, new_values,
        block_in, drift_in, gain, expert_ids,
    )
    attended = second_attention(
        lengths, drift_rows, queries, cache_keys, cache_values, new_keys, new_values
    )

    weights = (keep_in_vmem(own), keep_in_vmem(paired))

    def experts(send, first):
        rows = lax.all_to_all(send, "exp", split_axis=0, concat_axis=0, tiled=True)
        rows, first = lax.optimization_barrier((rows, first))
        size = SLOTS // VISITS
        visiting = [lax.ppermute(rows[i * size : (i + 1) * size], axes, across) for i in range(VISITS)]
        away_terms = [lax.ppermute(expert_half(part, weights), axes, across) for part in visiting]
        terms = expert_half(rows, weights)
        for i, away in enumerate(away_terms):
            terms = add_part(terms, away, i)
        return lax.all_to_all(terms, "exp", split_axis=0, concat_axis=0, tiled=True), first

    terms, (_, attended, gates, places) = experts(
        send, (paired, attended, gates, slot_places(expert_ids))
    )
    output, residual, send = combine_and_dispatch(
        terms, residual, attended, drift_in, gain, places, gates
    )
    terms, _ = experts(send, ())
    return combine_last(terms, residual, output, places, gates)


def solution(mesh):
    placed = (
        P(("rep", "exp"), None, None),
        P(("rep", "exp"), None, None),
        P(("rep", "exp")),
        P(None, ("rep", "exp"), None),
        P(("rep", "exp"), None, None),
        P(None, ("rep", "exp"), None, None),
        P(None, ("rep", "exp"), None, None),
        P(None, ("rep", "exp"), None, None),
        P(None, ("rep", "exp"), None, None),
        P(),
        P(None, ("rep", "exp"), None, None),
        P(None, ("rep", "exp"), None, None),
        P("exp", None, "rep"),
        P("exp", None, "rep"),
        P("exp", "rep", None),
    )
    return jax.shard_map(
        on_device,
        mesh=mesh,
        in_specs=placed,
        out_specs=P(None, ("rep", "exp"), None, None),
        check_vma=False,
    )
```

```python
import jax
import jax.numpy as jnp
from jax import lax
from jax.experimental import pallas as pl
from jax.experimental.pallas import tpu as pltpu
from jax.sharding import PartitionSpec as P

H = 32
KVH = 4
GROUP = H // KVH
HD = 128
D = H * HD
TOP = 8
BLOCK = 8
ROWS = 16
CAP = 3
EXPERTS = 64
SLOTS = EXPERTS * CAP
CACHE = 2048
QUARTER = 256
VISITS = 3
NEG = -1e30
VMEM_LIMIT = 24 * 1024 * 1024


def smem_spec():
    return pl.BlockSpec(memory_space=pltpu.SMEM)


def each_slot(ids_ref, denoise, counts, visit):
    for e in range(EXPERTS):
        counts[e] = 0

    @pl.loop(0, ROWS)
    def _(t):
        picked = []
        for j in range(TOP):
            e = ids_ref[denoise, 0, j, t]
            c = counts[e]
            counts[e] = c + 1
            picked.append(e * CAP + jnp.minimum(c, CAP - 1))
        visit(t, picked)


def slot_places(ids):
    def body(ids_ref, places_ref, counts):
        for denoise in range(2):

            def visit(t, picked):
                for j, slot in enumerate(picked):
                    places_ref[denoise, 0, j, t] = slot

            each_slot(ids_ref, denoise, counts, visit)

    return pl.pallas_call(
        body,
        in_specs=[smem_spec()],
        out_specs=smem_spec(),
        out_shape=jax.ShapeDtypeStruct(ids.shape, jnp.int32),
        scratch_shapes=[pltpu.SMEM((EXPERTS,), jnp.int32)],
        name="slot_places",
    )(ids)


def each_place(places_ref, denoise, visit):
    for t in range(ROWS):
        visit(t, [places_ref[denoise, 0, j, t] for j in range(TOP)])


def normalize(residual, gain):
    inverse = lax.rsqrt(jnp.mean(residual * residual, axis=-1, keepdims=True) + 1e-06)
    return residual * inverse * gain


def dispatch(normed, walk, spread, packed, send_ref):
    for k in range(H):
        spread[pl.ds(k, ROWS, stride=H), :] = normed[:, k * HD : (k + 1) * HD]
    packed[...] = spread[...].reshape(ROWS, H, HD).astype(jnp.bfloat16)
    send_ref[...] = jnp.zeros_like(send_ref)

    def visit(t, picked):
        row = packed[t]
        for slot in picked:
            send_ref[slot] = row

    walk(visit)


def combine(terms_ref, places_ref, gates_ref, denoise, spread):
    def visit(t, picked):
        shares = [
            gates_ref[denoise, 0, j, t] * terms_ref[slot].astype(jnp.float32)
            for j, slot in enumerate(picked)
        ]
        while len(shares) > 1:
            shares = [a + b for a, b in zip(shares[::2], shares[1::2])]
        spread[t * H : (t + 1) * H, :] = shares[0]

    each_place(places_ref, denoise, visit)
    return jnp.concatenate([spread[pl.ds(k, ROWS, stride=H), :] for k in range(H)], axis=1)


def attend_head(denoise, lengths_ref, drift_ref, q_ref, k_ref, v_ref, nk_ref, nv_ref, bias, attended):
    head = pl.program_id(0)
    extra = ROWS * (denoise + 1)

    @pl.when(head == 0)
    def _():
        place = lax.broadcasted_iota(jnp.int32, (1, CACHE), 1)
        admitted = place < lengths_ref[0]
        for step in range(denoise + 1):
            for b in range(BLOCK):
                admitted = admitted & (place != drift_ref[step, 0, b])
        bias[...] = jnp.where(admitted, 0.0, NEG)

    queries = jnp.concatenate([q_ref[:, g * HD : (g + 1) * HD] for g in range(GROUP)], axis=0)
    contract_last = (((1,), (1,)), ((), ()))
    scale = HD ** (-0.5)
    scores = lax.dot_general(queries, k_ref[...], contract_last, preferred_element_type=jnp.float32)
    scores = scores * scale + bias[...]
    fresh_k = nk_ref[0 : denoise + 1].reshape(extra, HD)
    fresh_v = nv_ref[0 : denoise + 1].reshape(extra, HD)
    fresh = lax.dot_general(queries, fresh_k, contract_last, preferred_element_type=jnp.float32)
    row = lax.broadcasted_iota(jnp.int32, (GROUP * ROWS, extra), 0)
    col = lax.broadcasted_iota(jnp.int32, (GROUP * ROWS, extra), 1)
    place = col % ROWS
    allowed = (col >= denoise * ROWS) & ((place >= BLOCK) | (row % ROWS < BLOCK))
    if denoise == 1:
        for b in range(BLOCK):
            kept = drift_ref[1, 0, 0] != drift_ref[0, 0, b]
            for other in range(1, BLOCK):
                kept = kept & (drift_ref[1, 0, other] != drift_ref[0, 0, b])
            allowed = allowed | ((col == BLOCK + b) & kept)
    fresh = jnp.where(allowed, fresh * scale, NEG)
    peak = jnp.maximum(
        jnp.max(scores, axis=-1, keepdims=True), jnp.max(fresh, axis=-1, keepdims=True)
    )
    scores = jnp.exp(scores - peak)
    fresh = jnp.exp(fresh - peak)
    denom = jnp.sum(scores, axis=-1, keepdims=True) + jnp.sum(fresh, axis=-1, keepdims=True)
    mixed = jnp.dot(scores.astype(jnp.bfloat16), v_ref[...], preferred_element_type=jnp.float32)
    mixed = mixed + jnp.dot(fresh.astype(jnp.bfloat16), fresh_v, preferred_element_type=jnp.float32)
    mixed = mixed / denom
    wide = jnp.concatenate([mixed[g * ROWS : (g + 1) * ROWS] for g in range(GROUP)], axis=1)
    attended[:, pl.ds(pl.multiple_of(head * GROUP * HD, GROUP * HD), GROUP * HD)] = wide


def attention_specs(denoise):
    return [
        smem_spec(),
        smem_spec(),
        pl.BlockSpec((None, None, ROWS, GROUP * HD), lambda h: (denoise, 0, 0, h)),
        pl.BlockSpec((None, CACHE, HD), lambda h: (0, 0, h)),
        pl.BlockSpec((None, CACHE, HD), lambda h: (0, 0, h)),
        pl.BlockSpec((2, None, ROWS, HD), lambda h: (0, 0, 0, h)),
        pl.BlockSpec((2, None, ROWS, HD), lambda h: (0, 0, 0, h)),
    ]


def first_attention(lengths, drift_rows, queries, keys, values, new_keys, new_values, block_in, drift_in, gain, ids):
    def body(lengths_ref, drift_ref, q_ref, k_ref, v_ref, nk_ref, nv_ref, block_ref, drift_in_ref, gain_ref, ids_ref,
             residual_ref, send_ref, bias, attended, spread, packed, counts):
        attend_head(0, lengths_ref, drift_ref, q_ref, k_ref, v_ref, nk_ref, nv_ref, bias, attended)

        @pl.when(pl.program_id(0) == KVH - 1)
        def _():
            inputs = jnp.concatenate(
                [block_ref[...].astype(jnp.float32), drift_in_ref[...].astype(jnp.float32)], axis=0
            )
            residual = inputs + attended[...]
            residual_ref[...] = residual
            walk = lambda visit: each_slot(ids_ref, 0, counts, visit)
            dispatch(normalize(residual, gain_ref[...]), walk, spread, packed, send_ref)

    return pl.pallas_call(
        body,
        grid=(KVH,),
        in_specs=attention_specs(0)
        + [
            pl.BlockSpec((None, BLOCK, D), lambda h: (0, 0, 0)),
            pl.BlockSpec((None, None, BLOCK, D), lambda h: (0, 0, 0, 0)),
            pl.BlockSpec((1, D), lambda h: (0, 0)),
            smem_spec(),
        ],
        out_specs=[
            pl.BlockSpec((ROWS, D), lambda h: (0, 0)),
            pl.BlockSpec((SLOTS, H, HD), lambda h: (0, 0, 0)),
        ],
        out_shape=[
            jax.ShapeDtypeStruct((ROWS, D), jnp.float32),
            jax.ShapeDtypeStruct((SLOTS, H, HD), jnp.bfloat16),
        ],
        scratch_shapes=[
            pltpu.VMEM((1, CACHE), jnp.float32),
            pltpu.VMEM((ROWS, D), jnp.float32),
            pltpu.VMEM((ROWS * H, HD), jnp.float32),
            pltpu.VMEM((ROWS, H, HD), jnp.bfloat16),
            pltpu.SMEM((EXPERTS,), jnp.int32),
        ],
        compiler_params=pltpu.CompilerParams(vmem_limit_bytes=56 * 1024 * 1024),
        name="first_attention",
    )(lengths, drift_rows, queries, keys, values, new_keys, new_values, block_in, drift_in, gain, ids)


def second_attention(lengths, drift_rows, queries, keys, values, new_keys, new_values):
    def body(lengths_ref, drift_ref, q_ref, k_ref, v_ref, nk_ref, nv_ref, attended, bias):
        attend_head(1, lengths_ref, drift_ref, q_ref, k_ref, v_ref, nk_ref, nv_ref, bias, attended)

    return pl.pallas_call(
        body,
        grid=(KVH,),
        in_specs=attention_specs(1),
        out_specs=pl.BlockSpec((ROWS, D), lambda h: (0, 0)),
        out_shape=jax.ShapeDtypeStruct((ROWS, D), jnp.float32),
        scratch_shapes=[pltpu.VMEM((1, CACHE), jnp.float32)],
        compiler_params=pltpu.CompilerParams(vmem_limit_bytes=VMEM_LIMIT),
        name="second_attention",
    )(lengths, drift_rows, queries, keys, values, new_keys, new_values)


def keep_in_vmem(weights):
    downs = weights[2:]
    shapes = (weights[0].shape, weights[1].shape, (sum(part.shape[0] for part in downs), D))

    def body(*refs):
        sources, (gate, up, down), sems = refs[: len(weights)], refs[len(weights) : -1], refs[-1]
        targets, row = [gate, up], 0
        for part in downs:
            targets.append(down.at[row : row + part.shape[0]])
            row += part.shape[0]
        copies = [
            pltpu.make_async_copy(source, target, sems.at[i])
            for i, (source, target) in enumerate(zip(sources, targets))
        ]
        for copy in copies:
            copy.start()
        for copy in copies:
            copy.wait()

    return pl.pallas_call(
        body,
        in_specs=[pl.BlockSpec(memory_space=pl.ANY)] * len(weights),
        out_specs=[pl.BlockSpec(memory_space=pltpu.VMEM)] * 3,
        out_shape=[pltpu.VMEM(shape, jnp.bfloat16) for shape in shapes],
        scratch_shapes=[pltpu.SemaphoreType.DMA((len(weights),))],
        compiler_params=pltpu.CompilerParams(vmem_limit_bytes=VMEM_LIMIT),
        name="keep_in_vmem",
    )(*weights)


def expert_half(rows, weights):
    pieces, count = len(weights), rows.shape[0]

    def body(*refs):
        rows_ref, weight_refs = refs[0], refs[1 : 1 + 3 * pieces]
        out_ref, flat, hidden = refs[1 + 3 * pieces :]
        for r in range(0, count, 16):
            wide = rows_ref[r : r + 16].astype(jnp.float32).reshape(16, D)
            flat[r : r + 16, :] = wide.astype(jnp.bfloat16)
        for p in range(pieces):
            gated = jnp.dot(flat[...], weight_refs[3 * p][...], preferred_element_type=jnp.float32)
            raised = jnp.dot(flat[...], weight_refs[3 * p + 1][...], preferred_element_type=jnp.float32)
            hidden[p] = (jax.nn.silu(gated) * raised).astype(jnp.bfloat16)
        width = 512
        heads = width // HD
        for n in range(D // width):
            part = jnp.zeros((count, width), jnp.float32)
            for p in range(pieces):
                part = part + jnp.dot(
                    hidden[p],
                    weight_refs[3 * p + 2][:, n * width : (n + 1) * width],
                    preferred_element_type=jnp.float32,
                )
            out_ref[:, n * heads : (n + 1) * heads, :] = part.reshape(count, heads, HD).astype(jnp.bfloat16)

    vmem = pl.BlockSpec(memory_space=pltpu.VMEM)
    return pl.pallas_call(
        body,
        in_specs=[vmem] * (1 + 3 * pieces),
        out_specs=vmem,
        out_shape=jax.ShapeDtypeStruct((count, H, HD), jnp.bfloat16),
        scratch_shapes=[
            pltpu.VMEM((count, D), jnp.bfloat16),
            pltpu.VMEM((pieces, count, QUARTER), jnp.bfloat16),
        ],
        compiler_params=pltpu.CompilerParams(vmem_limit_bytes=VMEM_LIMIT),
        name="expert_half",
    )(rows, *[part for piece in weights for part in piece])


def add_part(terms, away, part):
    steps = 2
    size = away.shape[0] // steps
    block = (size, H, HD)

    def body(terms_ref, away_ref, out_ref):
        total = terms_ref[...].astype(jnp.float32) + away_ref[...].astype(jnp.float32)
        out_ref[...] = total.astype(jnp.bfloat16)

    return pl.pallas_call(
        body,
        grid=(steps,),
        in_specs=[
            pl.BlockSpec(block, lambda i: (part * steps + i, 0, 0)),
            pl.BlockSpec(block, lambda i: (i, 0, 0)),
        ],
        out_specs=pl.BlockSpec(block, lambda i: (part * steps + i, 0, 0)),
        out_shape=jax.ShapeDtypeStruct(terms.shape, terms.dtype),
        input_output_aliases={0: 0},
        compiler_params=pltpu.CompilerParams(vmem_limit_bytes=VMEM_LIMIT),
        name="add_part",
    )(terms, away)


def combine_and_dispatch(terms, residual, attended, drift_in, gain, places, gates):
    def body(terms_ref, residual_ref, attended_ref, drift_in_ref, gain_ref, places_ref, gates_ref,
             out_ref, next_ref, send_ref, spread, packed):
        moe = combine(terms_ref, places_ref, gates_ref, 0, spread)
        result = (residual_ref[...] + moe).astype(jnp.bfloat16)
        out_ref[0, 0] = result
        inputs = jnp.concatenate(
            [result.astype(jnp.float32)[:BLOCK], drift_in_ref[1, 0].astype(jnp.float32)], axis=0
        )
        following = inputs + attended_ref[...]
        next_ref[...] = following
        walk = lambda visit: each_place(places_ref, 1, visit)
        dispatch(normalize(following, gain_ref[...]), walk, spread, packed, send_ref)

    vmem = pl.BlockSpec(memory_space=pltpu.VMEM)
    first_half = pl.BlockSpec((1, 1, ROWS, D), lambda i: (0, 0, 0, 0))
    return pl.pallas_call(
        body,
        grid=(1,),
        in_specs=[vmem] * 5 + [smem_spec()] * 2,
        out_specs=[first_half, vmem, vmem],
        out_shape=[
            jax.ShapeDtypeStruct((2, 1, ROWS, D), jnp.bfloat16),
            jax.ShapeDtypeStruct((ROWS, D), jnp.float32),
            jax.ShapeDtypeStruct((SLOTS, H, HD), jnp.bfloat16),
        ],
        scratch_shapes=[
            pltpu.VMEM((ROWS * H, HD), jnp.float32),
            pltpu.VMEM((ROWS, H, HD), jnp.bfloat16),
        ],
        compiler_params=pltpu.CompilerParams(vmem_limit_bytes=VMEM_LIMIT),
        name="combine_and_dispatch",
    )(terms, residual, attended, drift_in, gain, places, gates)


def combine_last(terms, residual, output, places, gates):
    def body(terms_ref, residual_ref, output_ref, places_ref, gates_ref, out_ref, spread):
        moe = combine(terms_ref, places_ref, gates_ref, 1, spread)
        out_ref[0, 0] = (residual_ref[...] + moe).astype(jnp.bfloat16)

    vmem = pl.BlockSpec(memory_space=pltpu.VMEM)
    return pl.pallas_call(
        body,
        grid=(1,),
        in_specs=[vmem] * 2 + [pl.BlockSpec(memory_space=pl.ANY)] + [smem_spec()] * 2,
        out_specs=pl.BlockSpec((1, 1, ROWS, D), lambda i: (1, 0, 0, 0)),
        out_shape=jax.ShapeDtypeStruct(output.shape, output.dtype),
        input_output_aliases={2: 0},
        scratch_shapes=[pltpu.VMEM((ROWS * H, HD), jnp.float32)],
        compiler_params=pltpu.CompilerParams(vmem_limit_bytes=VMEM_LIMIT),
        name="combine_last",
    )(terms, residual, output, places, gates)


def pairings(reps, exps):
    across, beside = [], []
    for r in range(reps):
        for e in range(exps):
            near, far = r ^ 1, reps - 1 - r
            if e % 2:
                near, far = far, near
            beside.append((r * exps + e, near * exps + e))
            across.append((r * exps + e, far * exps + e))
    return beside, across


def on_device(
    cache_keys,
    cache_values,
    lengths,
    drift_rows,
    block_in,
    drift_in,
    queries,
    new_keys,
    new_values,
    norm_gain,
    expert_ids,
    gate_weights,
    w_gate,
    w_up,
    w_down,
):
    axes = ("rep", "exp")
    beside, across = pairings(lax.axis_size("rep"), lax.axis_size("exp"))
    own = (w_gate[0], w_up[0], w_down[0])
    gate_up = [lax.ppermute(part, axes, beside) for part in own[:2]]
    downs = []
    for i, half in enumerate(jnp.split(own[2], 2)):
        gate_up[i], half = lax.optimization_barrier((gate_up[i], half))
        downs.append(lax.ppermute(half, axes, beside))
    paired = (*gate_up, *downs)
    gain = norm_gain.reshape(1, D)
    expert_ids = jnp.swapaxes(expert_ids, 2, 3)
    gates = jnp.swapaxes(gate_weights, 2, 3).astype(jnp.float32)

    residual, send = first_attention(
        lengths, drift_rows, queries, cache_keys, cache_values, new_keys, new_values,
        block_in, drift_in, gain, expert_ids,
    )
    attended = second_attention(
        lengths, drift_rows, queries, cache_keys, cache_values, new_keys, new_values
    )

    weights = (keep_in_vmem(own), keep_in_vmem(paired))

    def experts(send, first):
        rows = lax.all_to_all(send, "exp", split_axis=0, concat_axis=0, tiled=True)
        rows, first = lax.optimization_barrier((rows, first))
        size = SLOTS // VISITS
        visiting = [lax.ppermute(rows[i * size : (i + 1) * size], axes, across) for i in range(VISITS)]
        away_terms = [lax.ppermute(expert_half(part, weights), axes, across) for part in visiting]
        terms = expert_half(rows, weights)
        for i, away in enumerate(away_terms):
            terms = add_part(terms, away, i)
        return lax.all_to_all(terms, "exp", split_axis=0, concat_axis=0, tiled=True), first

    terms, (_, attended, gates, places) = experts(
        send, (paired, attended, gates, slot_places(expert_ids))
    )
    output, residual, send = combine_and_dispatch(
        terms, residual, attended, drift_in, gain, places, gates
    )
    terms, _ = experts(send, ())
    return combine_last(terms, residual, output, places, gates)


def solution(mesh):
    placed = (
        P(("rep", "exp"), None, None),
        P(("rep", "exp"), None, None),
        P(("rep", "exp")),
        P(None, ("rep", "exp"), None),
        P(("rep", "exp"), None, None),
        P(None, ("rep", "exp"), None, None),
        P(None, ("rep", "exp"), None, None),
        P(None, ("rep", "exp"), None, None),
        P(None, ("rep", "exp"), None, None),
        P(),
        P(None, ("rep", "exp"), None, None),
        P(None, ("rep", "exp"), None, None),
        P("exp", None, "rep"),
        P("exp", None, "rep"),
        P("exp", "rep", None),
    )
    return jax.shard_map(
        on_device,
        mesh=mesh,
        in_specs=placed,
        out_specs=P(None, ("rep", "exp"), None, None),
        check_vma=False,
    )
```
